32 devices in a mesh: dp: 16 (over z, y, x), tensor: 2 (over core).
Axes of the slice: x: 2, y: 2, z: 4, core: 2. Of those that a mesh axis runs over, the one named last changes fastest.
Arguments:
- tokens: bfloat16 [2048, 768], P('dp'), may hold values from -6 to 6
- cotangent: bfloat16 [2048, 768], P('dp'), may hold values from -6 to 6
- lengths: int32 [32], replicated, may hold values from 1 to 64, as said below
- owners: int32 [32], replicated, may hold values from 0 to 15, as said below
- w_qkv: bfloat16 [2, 3, 768, 768], P(None, None, 'dp', 'tensor')
- bias_qv: bfloat16 [2, 2, 2, 384], P(None, None, 'tensor', 'dp'), may hold values from -3 to 3
- w_out: bfloat16 [2, 2, 384, 768], P(None, 'tensor', 'dp'), may hold values from -0.625 to 0.625
- w_up: bfloat16 [2, 768, 3072], P(None, 'dp', 'tensor'), may hold values from -0.21875 to 0.21875
- bias_up: bfloat16 [2, 2, 1536], P(None, 'tensor', 'dp'), may hold values from 1.5 to 3
- w_down: bfloat16 [2, 2, 1536, 768], P(None, 'tensor', 'dp'), may hold values from -0.0546875 to 0.0546875
- vectors: bfloat16 [2, 6, 768], P(None, None, 'dp')
Outputs:
- output: float32 [2048, 768], P('dp')
- tokens_grad: float32 [2048, 768], P('dp')
- w_qkv_grad: float32 [2, 3, 768, 768], P(None, None, 'dp', 'tensor')
- bias_qv_grad: float32 [2, 2, 2, 384], P(None, None, 'tensor', 'dp')
- w_out_grad: float32 [2, 2, 384, 768], P(None, 'tensor', 'dp')
- w_up_grad: float32 [2, 768, 3072], P(None, 'dp', 'tensor')
- bias_up_grad: float32 [2, 2, 1536], P(None, 'tensor', 'dp')
- w_down_grad: float32 [2, 2, 1536, 768], P(None, 'tensor', 'dp')
- vectors_grad: float32 [2, 6, 768], P(None, None, 'dp')
The draws below stay inside these ranges and needn't reach their ends.
Inputs may be any that keep to these rules, and one draw needn't show every extreme that they name: `lengths`: the sequences of one index of dp hold at most 128 tokens in all, and those of some index exactly 128. `owners`: each index of dp holds exactly 2 sequences.
All inputs are finite; a program needn't handle non-finite values.
Results may differ from the reference program's by a relative error of at most 0.024.
Values may be sent and summed in bfloat16 or wider, within the bound.
No kernel may reach another device: no remote copies, remote signals or barrier semaphores. Data moves between devices by JAX's collectives and lax.ppermute only.
A program may use at most 192 MiB of HBM per device.

```python
import jax
import jax.numpy as jnp
from jax import lax

D = 768
HD = 64
FF = 3072
LAYERS = 2
MAXLEN = 64
SEQ_DEV = 2
CAP = 128
SEQS = 32
TOKENS = 2048
N_DP = 16
N_TENSOR = 2


def deal_sequences(key):
    order_key, size_key, full_key = jax.random.split(jax.random.fold_in(key, 11), 3)
    device_count = SEQS // SEQ_DEV
    owners = (jax.random.permutation(order_key, SEQS) // SEQ_DEV).astype(jnp.int32)
    lengths = jax.random.randint(size_key, (SEQS,), 1, MAXLEN + 1, dtype=jnp.int32)
    fullest = jax.random.randint(full_key, (), 0, device_count, dtype=jnp.int32)
    lengths = jnp.where(owners == fullest, MAXLEN, lengths).astype(jnp.int32)
    return (lengths, owners)


def draw_lengths(key, part):
    lengths, owners = deal_sequences(key)
    return lengths


def draw_owners(key, part):
    lengths, owners = deal_sequences(key)
    return owners


def draw_w_qkv(key, part):
    base = jax.random.normal(key, (LAYERS, 3, D, D), jnp.float32) * D ** (-0.5)
    return base.astype(jnp.bfloat16)


def draw_vectors(key, part):
    noise = jax.random.normal(key, (LAYERS, 6, D), jnp.float32)
    is_gain = jnp.array([1.0, 0.0, 0.0, 1.0, 0.0, 0.0], jnp.float32).reshape(1, 6, 1)
    values = is_gain * (1.0 + 0.15 * noise) + (1.0 - is_gain) * 0.3 * noise
    return values.astype(jnp.bfloat16)


def strengthened(values, rng, source, target, parts, factor):
    owner, partner = [(jnp.arange(values.shape[dim]) // (values.shape[dim] // parts)).reshape([-1 if axis == dim else 1 for axis in range(values.ndim)]) for dim in (source, target)]
    chosen = jax.random.permutation(rng, parts)[partner]
    strong = (owner == chosen) | (owner == (partner + parts // 2) % parts)
    return jnp.where(strong, factor * values, values)


def level_of(own_key, shape, pieces, least, high):
    level = 1.0
    for dim, blocks in pieces:
        draws = jax.random.uniform(jax.random.fold_in(jax.random.fold_in(own_key, 6), dim), (blocks,), jnp.float32, least / len(pieces), high / len(pieces))
        level = level * jnp.repeat(jnp.exp(draws), shape[dim] // blocks).reshape((-1,) + (1,) * (len(shape) - 1 - dim))
    return level


def bell_draw(key, extent, width, limit, cuts=(), kind=jnp.bfloat16):
    level = level_of(key, extent, cuts, -0.22, 0.18) if cuts else 1.0
    values = jax.random.normal(key, extent, jnp.float32) * width * level
    return jnp.minimum(jnp.maximum(values, -limit), limit).astype(kind)


def bell_draw_with(own_key, extent, deviation, bound, cuts, heavy, kind=jnp.bfloat16):
    entries = deviation * jax.random.normal(own_key, extent, jnp.float32)
    if cuts:
        entries = entries * level_of(own_key, extent, cuts, -0.22, 0.18)
    return jnp.clip(strengthened(entries, jax.random.fold_in(own_key, 3), *heavy), -bound, bound).astype(kind)


def setup_inputs(seed: int = 0) -> dict:
    streams_of = jax.random.split(jax.random.key(seed), 12)
    tokens = bell_draw(streams_of[0], (TOKENS, D), 1.0, 6.0, ((0, 16),))
    cotangent = bell_draw_with(streams_of[1], (TOKENS, D), 1.0, 6.0, ((0, 16),), (0, 1, 16, 2.0))
    lengths = draw_lengths(jax.random.fold_in(streams_of[11], 71), 0)
    owners = draw_owners(jax.random.fold_in(streams_of[11], 71), 0)
    w_qkv = draw_w_qkv(jax.random.fold_in(streams_of[11], 71), 0)
    bias_qv = bell_draw(streams_of[5], (LAYERS, 2, N_TENSOR, D // N_TENSOR), 0.5, 3.0, ((2, 2), (3, 16)))
    w_out = bell_draw(streams_of[6], (LAYERS, N_TENSOR, D // N_TENSOR, D), (D // 8) ** -0.5, 0.625, ((1, 2), (2, 16)))
    w_up = bell_draw(streams_of[7], (LAYERS, D, FF), D ** -0.5, 0.21875, ((1, 16), (2, 2)))
    bias_up = jnp.clip(1.5 + 1.5 * jax.random.uniform(streams_of[8], (LAYERS, N_TENSOR, FF // N_TENSOR), jnp.float32) ** level_of(streams_of[8], (LAYERS, N_TENSOR, FF // N_TENSOR), ((1, 2), (2, 16)), -0.2, 0.2), 1.5, 3.0).astype(jnp.bfloat16)
    w_down = bell_draw(streams_of[9], (LAYERS, N_TENSOR, FF // N_TENSOR, D), (4 * FF) ** -0.5, 0.0546875, ((1, 2), (2, 16)))
    vectors = draw_vectors(jax.random.fold_in(streams_of[11], 71), 0)
    return {"tokens": tokens, "cotangent": cotangent, "lengths": lengths, "owners": owners, "w_qkv": w_qkv, "bias_qv": bias_qv, "w_out": w_out, "w_up": w_up, "bias_up": bias_up, "w_down": w_down, "vectors": vectors}


epsilon = 1e-05
masked_score = -1e+30

def to_float(array):
    return array.astype(jnp.float32)

def slot_segments(lengths, owners, device, capacity):
    is_mine = owners == device
    owned_sizes = jnp.where(is_mine, lengths, 0).astype(jnp.int32)
    slot_begin = (jnp.cumsum(owned_sizes) - owned_sizes).astype(jnp.int32)
    slot_ids = jnp.arange(capacity, dtype=jnp.int32)
    slot_end = (slot_begin + owned_sizes).astype(jnp.int32)
    inside = is_mine[None, :] & (slot_ids[:, None] >= slot_begin[None, :]) & (slot_ids[:, None] < slot_end[None, :])
    sequence_ids = jnp.arange(lengths.shape[0], dtype=jnp.int32)
    matched = lax.optimization_barrier(jnp.sum(jnp.where(inside, sequence_ids[None, :] + 1, 0), axis=1)).astype(jnp.int32)
    return jnp.where(matched > 0, matched - 1, lengths.shape[0] + slot_ids).astype(jnp.int32)

def norm_forward(hidden, gain_row, shift_row):
    mean_row = lax.optimization_barrier(jnp.mean(hidden, axis=-1, keepdims=True))
    centered = hidden - mean_row
    inverse = lax.rsqrt(lax.optimization_barrier(jnp.mean(centered * centered, axis=-1, keepdims=True)) + epsilon)
    normal_hat = centered * inverse
    return (normal_hat * gain_row + shift_row, normal_hat, inverse)

def norm_backward(incoming, normal_hat, inverse, gain_row):
    gain_grad = lax.optimization_barrier(jnp.sum(incoming * normal_hat, axis=0))
    shift_grad = lax.optimization_barrier(jnp.sum(incoming, axis=0))
    scaled = incoming * gain_row
    back = inverse * (scaled - lax.optimization_barrier(jnp.mean(scaled, axis=-1, keepdims=True)) - normal_hat * lax.optimization_barrier(jnp.mean(scaled * normal_hat, axis=-1, keepdims=True)))
    return (back, gain_grad, shift_grad)

def block_scores(query_block, key_rows, segment_ids, row_start):
    block_rows, head_count, head_size = query_block.shape
    scores = jnp.einsum('qhd,khd->hqk', to_float(query_block), to_float(key_rows)) * head_size ** (-0.5)
    row_ids = row_start + jnp.arange(block_rows, dtype=jnp.int32)
    column_ids = jnp.arange(key_rows.shape[0], dtype=jnp.int32)
    block_segments = lax.dynamic_slice_in_dim(segment_ids, row_start, block_rows, 0)
    allowed = (block_segments[:, None] == segment_ids[None, :]) & (column_ids[None, :] <= row_ids[:, None])
    return jnp.where(allowed[None], scores, masked_score)

def attend(query_rows, key_rows, value_rows, segment_ids):
    capacity = query_rows.shape[0]
    block_rows = min(capacity, 512)

    def one_block(row_start):
        query_block = lax.dynamic_slice_in_dim(query_rows, row_start, block_rows, 0)
        scores = block_scores(query_block, key_rows, segment_ids, row_start)
        row_max = lax.optimization_barrier(jnp.max(scores, axis=-1, keepdims=True))
        log_total = row_max + jnp.log(lax.optimization_barrier(jnp.sum(jnp.exp(scores - row_max), axis=-1, keepdims=True)))
        softmax_low = jnp.exp(scores - log_total).astype(jnp.bfloat16)
        attended = jnp.einsum('hqk,khd->qhd', to_float(softmax_low), to_float(value_rows)).astype(jnp.bfloat16)
        return (attended, log_total[..., 0])
    block_starts = jnp.arange(capacity // block_rows, dtype=jnp.int32) * block_rows
    attended, log_total = lax.map(one_block, block_starts)
    return (attended.reshape(query_rows.shape), log_total)

def attend_back(query_rows, key_rows, value_rows, attended_grad, log_total, segment_ids):
    capacity, head_count, head_size = query_rows.shape
    block_rows = min(capacity, 512)

    def one_block(running, element):
        key_sum, value_sum = running
        row_start, total_block = element
        query_block = lax.dynamic_slice_in_dim(query_rows, row_start, block_rows, 0)
        grad_block = lax.dynamic_slice_in_dim(attended_grad, row_start, block_rows, 0)
        scores = block_scores(query_block, key_rows, segment_ids, row_start)
        softmax_rows = jnp.exp(scores - total_block[..., None])
        softmax_low = softmax_rows.astype(jnp.bfloat16)
        value_sum = value_sum + jnp.einsum('hqk,qhd->khd', to_float(softmax_low), to_float(grad_block))
        prob_grad = jnp.einsum('qhd,khd->hqk', to_float(grad_block), to_float(value_rows))
        row_dot = lax.optimization_barrier(jnp.sum(softmax_rows * prob_grad, axis=-1, keepdims=True))
        score_grad = (softmax_rows * (prob_grad - row_dot) * head_size ** (-0.5)).astype(jnp.bfloat16)
        query_grad = jnp.einsum('hqk,khd->qhd', to_float(score_grad), to_float(key_rows))
        key_sum = key_sum + jnp.einsum('hqk,qhd->khd', to_float(score_grad), to_float(query_block))
        return ((key_sum, value_sum), query_grad)
    block_starts = jnp.arange(capacity // block_rows, dtype=jnp.int32) * block_rows
    empty_grad = jnp.zeros(key_rows.shape, jnp.float32)
    (key_sum, value_sum), query_grad = lax.scan(one_block, (empty_grad, empty_grad), (block_starts, log_total))
    return (query_grad.reshape(query_rows.shape), key_sum, value_sum)

def layer_forward(hidden, params, segment_ids):
    qkv_weight, pair_bias, out_weight, up_weight, up_bias, down_weight, vector_rows = params
    normed, first_hat, first_inverse = norm_forward(hidden, vector_rows[0], vector_rows[1])
    normed_low = normed.astype(jnp.bfloat16)
    projected = jnp.einsum('td,cdf->ctf', to_float(normed_low), to_float(qkv_weight))
    shifts = jnp.stack([pair_bias[0], jnp.zeros_like(pair_bias[0]), pair_bias[1]])
    projected = (projected + shifts[:, None, :]).astype(jnp.bfloat16)
    capacity, local_width = (projected.shape[1], projected.shape[2])
    head_shape = (capacity, local_width // HD, HD)
    attended, log_total = attend(projected[0].reshape(head_shape), projected[1].reshape(head_shape), projected[2].reshape(head_shape), segment_ids)
    attended_flat = attended.reshape(capacity, local_width)
    middle = hidden + (jnp.dot(attended_flat, out_weight, preferred_element_type=jnp.float32) + vector_rows[2])
    second_normed, second_hat, second_inverse = norm_forward(middle, vector_rows[3], vector_rows[4])
    second_low = second_normed.astype(jnp.bfloat16)
    before = jnp.dot(second_low, up_weight, preferred_element_type=jnp.float32) + up_bias
    active = jnp.maximum(before, 0.0).astype(jnp.bfloat16)
    result = middle + (jnp.dot(active, down_weight, preferred_element_type=jnp.float32) + vector_rows[5])
    saved_state = (normed_low, first_hat, first_inverse, projected, attended_flat, log_total, second_hat, second_inverse, second_low, before, active)
    return (result, saved_state)

def layer_backward(incoming, params, saved_state, segment_ids):
    qkv_weight, pair_bias, out_weight, up_weight, up_bias, down_weight, vector_rows = params
    normed_low, first_hat, first_inverse, projected, attended_flat, log_total, second_hat, second_inverse, second_low, before, active = saved_state
    capacity, local_width = attended_flat.shape
    head_shape = (capacity, local_width // HD, HD)
    down_bias_grad = lax.optimization_barrier(jnp.sum(incoming, axis=0))
    incoming_low = incoming.astype(jnp.bfloat16)
    down_grad = jnp.dot(active.T, incoming_low, preferred_element_type=jnp.float32)
    active_grad = jnp.dot(incoming_low, down_weight.T, preferred_element_type=jnp.float32)
    before_grad = jnp.where(before > 0, active_grad, 0.0)
    up_bias_grad = lax.optimization_barrier(jnp.sum(before_grad, axis=0))
    before_low = before_grad.astype(jnp.bfloat16)
    up_grad = jnp.dot(second_low.T, before_low, preferred_element_type=jnp.float32)
    second_grad = jnp.dot(before_low, up_weight.T, preferred_element_type=jnp.float32)
    back_second, second_gain_grad, second_shift_grad = norm_backward(second_grad, second_hat, second_inverse, vector_rows[3])
    middle_grad = incoming + back_second
    out_bias_grad = lax.optimization_barrier(jnp.sum(middle_grad, axis=0))
    middle_low = middle_grad.astype(jnp.bfloat16)
    out_grad = jnp.dot(attended_flat.T, middle_low, preferred_element_type=jnp.float32)
    attended_grad = jnp.dot(middle_low, out_weight.T, preferred_element_type=jnp.float32).astype(jnp.bfloat16).reshape(head_shape)
    query_grad, key_grad, value_grad = attend_back(projected[0].reshape(head_shape), projected[1].reshape(head_shape), projected[2].reshape(head_shape), attended_grad, log_total, segment_ids)
    qkv_grad = jnp.stack([query_grad.reshape(capacity, local_width), key_grad.reshape(capacity, local_width), value_grad.reshape(capacity, local_width)])
    pair_grad = jnp.stack([lax.optimization_barrier(jnp.sum(qkv_grad[0], axis=0)), lax.optimization_barrier(jnp.sum(qkv_grad[2], axis=0))])
    qkv_low = qkv_grad.astype(jnp.bfloat16)
    weight_grad = jnp.einsum('td,ctf->cdf', to_float(normed_low), to_float(qkv_low))
    first_grad = jnp.einsum('ctf,cdf->td', to_float(qkv_low), to_float(qkv_weight))
    back_first, first_gain_grad, first_shift_grad = norm_backward(first_grad, first_hat, first_inverse, vector_rows[0])
    outgoing = middle_grad + back_first
    vector_grad = jnp.stack([first_gain_grad, first_shift_grad, out_bias_grad, second_gain_grad, second_shift_grad, down_bias_grad])
    return (outgoing, (weight_grad, pair_grad, out_grad, up_grad, up_bias_grad, down_grad, vector_grad))

def reference(tokens, cotangent, lengths, owners, w_qkv, bias_qv, w_out, w_up, bias_up, w_down, vectors):

    def layer_params(layer_index):
        return (w_qkv[layer_index], to_float(bias_qv[layer_index]).reshape(2, D), w_out[layer_index].reshape(D, D), w_up[layer_index], to_float(bias_up[layer_index]).reshape(FF), w_down[layer_index].reshape(FF, D), to_float(vectors[layer_index]))

    def device_step(totals, element):
        block_tokens, block_cotangent, device = element
        segment_ids = slot_segments(lengths, owners, device, block_tokens.shape[0])
        live_rows = (segment_ids < lengths.shape[0]).astype(jnp.float32)
        hidden = to_float(block_tokens)
        saved_list = []
        for layer_index in range(LAYERS):
            hidden, saved_state = layer_forward(hidden, layer_params(layer_index), segment_ids)
            saved_list.append(saved_state)
        incoming = to_float(block_cotangent) * live_rows[:, None]
        new_totals = list(totals)
        for layer_index in reversed(range(LAYERS)):
            incoming, layer_grads = layer_backward(incoming, layer_params(layer_index), saved_list[layer_index], segment_ids)
            for member in range(7):
                new_totals[member] = new_totals[member].at[layer_index].add(layer_grads[member])
        return (tuple(new_totals), (hidden, incoming))
    totals = (jnp.zeros((LAYERS, 3, D, D), jnp.float32), jnp.zeros((LAYERS, 2, D), jnp.float32), jnp.zeros((LAYERS, D, D), jnp.float32), jnp.zeros((LAYERS, D, FF), jnp.float32), jnp.zeros((LAYERS, FF), jnp.float32), jnp.zeros((LAYERS, FF, D), jnp.float32), jnp.zeros((LAYERS, 6, D), jnp.float32))
    blocks = (tokens.reshape(N_DP, CAP, D), cotangent.reshape(N_DP, CAP, D), jnp.arange(N_DP, dtype=jnp.int32))
    totals, (outputs, incoming) = lax.scan(device_step, totals, blocks)
    return (outputs.reshape(TOKENS, D), incoming.reshape(TOKENS, D), totals[0], totals[1].reshape(LAYERS, 2, N_TENSOR, D // N_TENSOR), totals[2].reshape(LAYERS, N_TENSOR, D // N_TENSOR, D), totals[3], totals[4].reshape(LAYERS, N_TENSOR, FF // N_TENSOR), totals[5].reshape(LAYERS, N_TENSOR, FF // N_TENSOR, D), totals[6])
```

```python
import jax
import jax.numpy as jnp
from jax import lax
from jax.experimental import pallas as pl
from jax.experimental.pallas import tpu as pltpu
from jax.sharding import PartitionSpec as P

HD = 64
epsilon = 1e-05
masked_score = -1e30
bf16 = jnp.bfloat16
f32 = jnp.float32


def slot_segments(lengths, owners, device, capacity):
    is_mine = owners == device
    owned_sizes = jnp.where(is_mine, lengths, 0)
    count = lengths.shape[0]
    order = jnp.arange(count, dtype=jnp.int32)
    before = order[None, :] < order[:, None]
    slot_begin = jnp.sum(jnp.where(before, owned_sizes[None, :], 0), axis=1)
    slot_ids = jnp.arange(capacity, dtype=jnp.int32)
    slot_end = slot_begin + owned_sizes
    inside = (
        is_mine[None, :]
        & (slot_ids[:, None] >= slot_begin[None, :])
        & (slot_ids[:, None] < slot_end[None, :])
    )
    matched = jnp.sum(jnp.where(inside, order[None, :] + 1, 0), axis=1)
    return jnp.where(matched > 0, matched - 1, count + slot_ids)


class Mover:
    def __init__(self, size):
        self.size = size
        self.lined = size == 16
        self.me = lax.axis_index("dp")
        if self.lined:
            self.bits = ((2, 1), (1, 2))
        else:
            high = [1 << k for k in range(2, size.bit_length() - 1)]
            low = [b for b in (2, 1) if b < size]
            self.bits = (tuple(high + low), tuple(high + low[::-1]))
        self.tables = tuple(self.table(half) for half in (0, 1))

    def xor(self, bit):
        return [(i, i ^ bit) for i in range(self.size)]

    def line(self, pairs):
        low = self.size // 4
        return [(a * low + r, b * low + r) for a, b in pairs for r in range(low)]

    def table(self, half):
        me = self.me
        if self.lined:
            z = me // 4
            first = z < 2
            zs = jnp.stack([z, z ^ 1, jnp.where(first, 2, 1), jnp.where(first, 3, 0)])
            spots = zs * 4 + me % 4
        else:
            spots = me[None]
        for bit in self.bits[half]:
            spots = jnp.concatenate([spots, spots ^ bit])
        return spots.astype(jnp.int32)

    def gather(self, block, half):
        held = block[None]
        if self.lined:
            near = jnp.concatenate([held, lax.ppermute(held, "dp", self.xor(4))])
            inner = lax.ppermute(near, "dp", self.line(((1, 2), (2, 1))))
            outer = lax.ppermute(inner, "dp", self.line(((1, 0), (2, 3))))
            z = self.me // 4
            is_inner = (z == 1) | (z == 2)
            held = jnp.concatenate([near, jnp.where(is_inner, inner, outer)])
        bits = self.bits[half]
        for bit in bits[:-1]:
            held = jnp.concatenate([held, lax.ppermute(held, "dp", self.xor(bit))])
        return held, lax.ppermute(held, "dp", self.xor(bits[-1]))

    def reduce(self, kept, sent, half, kind=bf16):
        bits = self.bits[half][::-1]
        back = lax.ppermute(sent, "dp", self.xor(bits[0]))
        keep = (kept, back)

        def total(pair, window):
            return pair[0][window].astype(f32) + pair[1][window].astype(f32)

        for bit in bits[1:]:
            middle = keep[0].shape[0] // 2
            out = total(keep, slice(middle, None)).astype(kind)
            back = lax.ppermute(out, "dp", self.xor(bit))
            keep = (total(keep, slice(0, middle)), back)
        if self.lined:
            far = total(keep, slice(2, 4))
            came = lax.ppermute(far.astype(kind), "dp", self.line(((0, 1), (3, 2))))
            far = far + came.astype(f32)
            came = lax.ppermute(far.astype(kind), "dp", self.line(((1, 2), (2, 1))))
            near_out = total(keep, slice(1, 2)) + came[1:2].astype(f32)
            near_own = total(keep, slice(0, 1)) + came[0:1].astype(f32)
            came = lax.ppermute(near_out.astype(kind), "dp", self.xor(4))
            return (near_own + came.astype(f32))[0]
        return total(keep, slice(0, 1))[0]

    def absolute(self, blocks, half):
        spots = self.tables[half]
        order = jnp.argsort(spots)
        return jnp.take(blocks, order, axis=0)


def pack_attention(w_qkv, w_out):
    wide = w_qkv.shape[-1]
    rows = w_out.shape[0]
    qk = w_qkv[:2]
    vo = jnp.concatenate(
        [
            w_qkv[2].reshape(2, rows, wide),
            jnp.stack([w_out[:, :wide], w_out[:, wide:]]),
        ]
    )
    return qk, vo


def unpack_attention(qk, vo):
    rows, wide = vo.shape[1:]
    qkv = jnp.concatenate([qk, vo[:2].reshape(1, 2 * rows, wide)])
    return qkv, jnp.concatenate([vo[2], vo[3]], axis=-1)


def dot(a, b):
    return lax.dot_general(a, b, (((1,), (0,)), ((), ())), preferred_element_type=f32)


def dot_t(a, b):
    return lax.dot_general(a, b, (((1,), (1,)), ((), ())), preferred_element_type=f32)


def t_dot(a, b):
    return lax.dot_general(a, b, (((0,), (0,)), ((), ())), preferred_element_type=f32)


def norm_parts(hidden):
    mean_row = jnp.mean(hidden, axis=-1, keepdims=True)
    centered = hidden - mean_row
    inverse = lax.rsqrt(jnp.mean(centered * centered, axis=-1, keepdims=True) + epsilon)
    return centered * inverse, inverse


def norm_backward(incoming, hat, inverse, gain_row):
    gain_grad = jnp.sum(incoming * hat, axis=0, keepdims=True)
    shift_grad = jnp.sum(incoming, axis=0, keepdims=True)
    scaled = incoming * gain_row
    back = inverse * (
        scaled
        - jnp.mean(scaled, axis=-1, keepdims=True)
        - hat * jnp.mean(scaled * hat, axis=-1, keepdims=True)
    )
    return back, gain_grad, shift_grad


class Fetch:
    def __init__(self, table, row, parts, places, sems):
        self.copies = []
        spot = 0
        for part in parts:
            for k in range(part.shape[0]):
                where = table[row, spot]
                for j, (pick, place) in enumerate(places):
                    self.copies.append(
                        pltpu.make_async_copy(
                            pick(part, k), place(where), sems.at[spot * len(places) + j]
                        )
                    )
                spot += 1
        for copy in self.copies:
            copy.start()

    def wait(self):
        for copy in self.copies:
            copy.wait()


class Deliver(Fetch):
    def __init__(self, table, row, parts, pick, sems):
        self.copies = []
        spot = 0
        for part in parts:
            for k in range(part.shape[0]):
                self.copies.append(
                    pltpu.make_async_copy(pick(table[row, spot]), part.at[k], sems.at[spot])
                )
                spot += 1
        for copy in self.copies:
            copy.start()


def attention_fetch(table, qk, vo, wqk, wvo, sem_a, sem_b):
    first = Fetch(table, 0, qk, [(lambda a, k: a.at[k], lambda d: wqk.at[d])], sem_a)
    second = Fetch(table, 1, vo, [(lambda a, k: a.at[k], lambda d: wvo.at[d])], sem_b)
    return first, second


def flat_rows(ref, picks):
    pieces = [ref[d, s].astype(f32) for d, s in picks]
    return jnp.concatenate(pieces, axis=0).astype(bf16)


def qk_weight(wqk, c):
    n = wqk.shape[0]
    return jnp.concatenate([wqk[d, c] for d in range(n)], axis=0)


def v_weight(wvo):
    return flat_rows(wvo, [(d, s) for d in range(wvo.shape[0]) for s in range(2)])


def out_weight(wvo, c):
    return flat_rows(wvo, [(d, 2 + c) for d in range(wvo.shape[0])])


def head_scores(q_pair, k_pair, mine, allowed):
    scores = dot_t(jnp.where(mine, q_pair, jnp.zeros_like(q_pair)), k_pair) * HD ** (-0.5)
    scores = jnp.where(allowed, scores, masked_score)
    row_max = jnp.max(scores, axis=-1, keepdims=True)
    lse = row_max + jnp.log(jnp.sum(jnp.exp(scores - row_max), axis=-1, keepdims=True))
    return jnp.exp(scores - lse)


def allowed_pairs(seg_col, seg_row):
    size = seg_col.shape[0]
    rows = lax.broadcasted_iota(jnp.int32, (size, size), 0)
    columns = lax.broadcasted_iota(jnp.int32, (size, size), 1)
    return (seg_col[...] == seg_row[...]) & (columns <= rows)


def lane_half(size):
    return lax.broadcasted_iota(jnp.int32, (size, 2 * HD), 1) < HD


def attention_forward_kernel(layer, parts, *refs):
    refs = list(refs)
    take = lambda n: [refs.pop(0) for _ in range(n)]
    (table,) = take(1)
    if layer == 0:
        (tokens,) = take(1)
    else:
        middle, own, other, before_vec = take(4)
    vec, bias, seg_col, seg_row = take(4)
    qk, vo = take(parts), take(parts)
    if layer:
        (hidden_out,) = take(1)
    normed_out, qkv_out, attended_out, partial_out = take(4)
    wqk, wvo, sem_a, sem_b = take(4)
    fetch_qk, fetch_vo = attention_fetch(table, qk, vo, wqk, wvo, sem_a, sem_b)
    if layer == 0:
        hidden = tokens[...].astype(f32)
    else:
        hidden = middle[...] + ((own[...] + other[...]) + before_vec[5:6, :])
        hidden_out[...] = hidden
    hat, inverse = norm_parts(hidden)
    normed = (hat * vec[0:1, :] + vec[1:2, :]).astype(bf16)
    normed_out[...] = normed
    allowed = allowed_pairs(seg_col, seg_row)
    low = lane_half(normed.shape[0])
    fetch_qk.wait()
    qkv_out[0] = (dot(normed, qk_weight(wqk, 0)) + bias[0:1, :]).astype(bf16)
    qkv_out[1] = dot(normed, qk_weight(wqk, 1)).astype(bf16)
    fetch_vo.wait()
    qkv_out[2] = (dot(normed, v_weight(wvo)) + bias[1:2, :]).astype(bf16)
    for pair in range(qkv_out.shape[2] // (2 * HD)):
        lanes = slice(pair * 2 * HD, (pair + 1) * 2 * HD)
        q, k, v = (qkv_out[c, :, lanes] for c in range(3))
        outs = []
        for mine in (low, ~low):
            probs = head_scores(q, k, mine, allowed)
            outs.append(dot(probs.astype(bf16), v))
        attended_out[:, lanes] = jnp.where(low, outs[0], outs[1]).astype(bf16)
    attended = attended_out[...]
    wide = attended.shape[1]
    for c in range(2):
        partial_out[:, c * wide : (c + 1) * wide] = dot(attended, out_weight(wvo, c))


def feed_forward(hidden, own, other, vec, bias_up, wup):
    middle = hidden + ((own + other) + vec[2:3, :])
    hat, inverse = norm_parts(middle)
    second = (hat * vec[3:4, :] + vec[4:5, :]).astype(bf16)
    active = jnp.maximum(dot(second, wup) + bias_up, 0.0).astype(bf16)
    return middle, second, active


def feed_backward(gb, second, active, wup, wdown, g_up, g_down, outs, table, sems):
    psec_out, dup, ddown, dbias_out = outs
    n, rows = g_down.shape[:2]
    act_grad = dot_t(gb, wdown)
    pre_grad = jnp.where(active > 0, act_grad, 0.0)
    dbias_out[...] = jnp.sum(pre_grad, axis=0, keepdims=True)
    pre_low = pre_grad.astype(bf16)
    g_up[...] = t_dot(second, pre_low).astype(bf16).reshape(g_up.shape)
    deliver_up = Deliver(table, 0, dup, lambda d: g_up.at[d], sems[0])
    g_down[...] = t_dot(active, gb).astype(bf16).reshape(g_down.shape)
    deliver_down = Deliver(table, 1, ddown, lambda d: g_down.at[d], sems[1])
    psec_out[...] = dot_t(pre_low, wup).astype(bf16)
    return deliver_up, deliver_down


def up_down_fetch(table, up, down, wup, wdown, sem_a, sem_b):
    one = [(lambda a, k: a.at[k], lambda d: wup.at[d])]
    two = [(lambda a, k: a.at[k], lambda d: wdown.at[d])]
    return Fetch(table, 0, up, one, sem_a), Fetch(table, 1, down, two, sem_b)


def merged(ref):
    value = ref[...]
    return value.reshape(value.shape[0] * value.shape[1], value.shape[2])


def ffn_forward_kernel(parts, table, hidden, own, other, vec, bias_up, *refs):
    refs = list(refs)
    take = lambda n: [refs.pop(0) for _ in range(n)]
    up, down = take(parts), take(parts)
    middle_out, second_out, active_out, partial_out = take(4)
    wup, wdown, sem_a, sem_b = take(4)
    fetch_up, fetch_down = up_down_fetch(table, up, down, wup, wdown, sem_a, sem_b)
    fetch_up.wait()
    middle, second, active = feed_forward(
        hidden[...].astype(f32), own[...], other[...], vec, bias_up[...], merged(wup)
    )
    middle_out[...] = middle
    second_out[...] = second
    active_out[...] = active
    fetch_down.wait()
    partial_out[...] = dot(active, merged(wdown))


def ffn_turn_kernel(
    parts, table, hidden, own, other, vec, bias_up, cotangent, live, *refs
):
    refs = list(refs)
    take = lambda n: [refs.pop(0) for _ in range(n)]
    up, down = take(parts), take(parts)
    middle_out, partial_out, psec_out, dbias_out, dshift_out = take(5)
    dup, ddown = take(parts), take(parts)
    wup, wdown, g_up, g_down, sem_a, sem_b, sem_c, sem_d = take(8)
    fetch_up, fetch_down = up_down_fetch(table, up, down, wup, wdown, sem_a, sem_b)
    g = cotangent[...].astype(f32) * live[...]
    dshift_out[...] = jnp.sum(g, axis=0, keepdims=True)
    fetch_up.wait()
    up_all = merged(wup)
    middle, second, active = feed_forward(
        hidden[...].astype(f32), own[...], other[...], vec, bias_up[...], up_all
    )
    middle_out[...] = middle
    fetch_down.wait()
    down_all = merged(wdown)
    delivered = feed_backward(
        g.astype(bf16), second, active, up_all, down_all, g_up, g_down,
        (psec_out, dup, ddown, dbias_out), table, (sem_c, sem_d),
    )
    partial_out[...] = dot(active, down_all)
    for one in delivered:
        one.wait()


def ffn_backward_kernel(
    parts, table, middle_grad, own, other, hidden, vec, second, active, *refs
):
    refs = list(refs)
    take = lambda n: [refs.pop(0) for _ in range(n)]
    up, down = take(parts), take(parts)
    g_out, psec_out, dbias_out, dshift_out, dnorm_out = take(5)
    dup, ddown = take(parts), take(parts)
    wup, wdown, g_up, g_down, sem_a, sem_b, sem_c, sem_d = take(8)
    fetch_up, fetch_down = up_down_fetch(table, up, down, wup, wdown, sem_a, sem_b)
    g = input_gradient(middle_grad, own, other, hidden, vec, dnorm_out)
    g_out[...] = g
    dshift_out[...] = jnp.sum(g, axis=0, keepdims=True)
    fetch_down.wait()
    fetch_up.wait()
    delivered = feed_backward(
        g.astype(bf16), second[...], active[...], merged(wup), merged(wdown), g_up, g_down,
        (psec_out, dup, ddown, dbias_out), table, (sem_c, sem_d),
    )
    for one in delivered:
        one.wait()


def input_gradient(middle_grad, own, other, hidden, vec, dnorm_out):
    first_grad = own[...].astype(f32) + other[...].astype(f32)
    hat, inverse = norm_parts(hidden[...].astype(f32))
    back, gain_grad, shift_grad = norm_backward(first_grad, hat, inverse, vec[0:1, :])
    dnorm_out[0:1, :] = gain_grad
    dnorm_out[1:2, :] = shift_grad
    return middle_grad[...] + back


def last_kernel(middle_grad, own, other, hidden, vec, grad_out, dnorm_out):
    grad_out[...] = input_gradient(middle_grad, own, other, hidden, vec, dnorm_out)


def attention_backward_kernel(layer, parts, *refs):
    refs = list(refs)
    take = lambda n: [refs.pop(0) for _ in range(n)]
    (table,) = take(1)
    if layer:
        cotangent, live = take(2)
    else:
        (g_in,) = take(1)
    own, other, middle, vec, attended_in, qkv, normed, seg_col, seg_row = take(9)
    qk, vo = take(parts), take(parts)
    middle_grad_out, pfirst_out, dbias_out, dnorm_out = take(4)
    dqk, dvo = take(parts), take(parts)
    wqk, wvo, g_qk, g_vo, low_ref, sem_a, sem_b, sem_c, sem_d = take(9)
    fetch_qk, fetch_vo = attention_fetch(table, qk, vo, wqk, wvo, sem_a, sem_b)
    if layer:
        g = cotangent[...].astype(f32) * live[...]
    else:
        g = g_in[...]
    second_grad = own[...].astype(f32) + other[...].astype(f32)
    hat, inverse = norm_parts(middle[...])
    back, gain_grad, shift_grad = norm_backward(second_grad, hat, inverse, vec[3:4, :])
    middle_grad = g + back
    middle_grad_out[...] = middle_grad
    dnorm_out[0:1, :] = jnp.sum(middle_grad, axis=0, keepdims=True)
    dnorm_out[1:2, :] = gain_grad
    dnorm_out[2:3, :] = shift_grad
    middle_low = middle_grad.astype(bf16)
    allowed = allowed_pairs(seg_col, seg_row)
    low = lane_half(middle_low.shape[0])
    n, _, rows, wide = g_vo.shape
    attended = attended_in[...]
    out_grad = t_dot(attended, middle_low)
    for c in range(2):
        part = out_grad[:, c * wide : (c + 1) * wide].reshape(n, rows, wide).astype(bf16)
        for d in range(n):
            g_vo[d, 2 + c] = part[d]
    fetch_vo.wait()
    attended_grad = dot_t(middle_low[:, :wide], out_weight(wvo, 0)) + dot_t(
        middle_low[:, wide:], out_weight(wvo, 1)
    )
    attended_grad = attended_grad.astype(bf16)
    scale = HD ** (-0.5)
    for pair in range(wide // (2 * HD)):
        lanes = slice(pair * 2 * HD, (pair + 1) * 2 * HD)
        q, k, v = (qkv[c, :, lanes] for c in range(3))
        da = attended_grad[:, lanes]
        dq, dk, dv = [], [], []
        for mine in (low, ~low):
            probs = head_scores(q, k, mine, allowed)
            dv.append(t_dot(probs.astype(bf16), da))
            dprob = dot_t(jnp.where(mine, da, jnp.zeros_like(da)), v)
            row_dot = jnp.sum(probs * dprob, axis=-1, keepdims=True)
            ds = (probs * (dprob - row_dot) * scale).astype(bf16)
            dq.append(dot(ds, k))
            dk.append(t_dot(ds, q))
        dq = jnp.where(low, dq[0], dq[1])
        dk = jnp.where(low, dk[0], dk[1])
        dv = jnp.where(low, dv[0], dv[1])
        dbias_out[0:1, lanes] = jnp.sum(dq, axis=0, keepdims=True)
        dbias_out[1:2, lanes] = jnp.sum(dv, axis=0, keepdims=True)
        low_ref[0, :, lanes] = dq.astype(bf16)
        low_ref[1, :, lanes] = dk.astype(bf16)
        low_ref[2, :, lanes] = dv.astype(bf16)
    a = normed[...]
    big = g_qk.shape[2]
    for c in range(2):
        part = t_dot(a, low_ref[c]).reshape(n, big, wide).astype(bf16)
        for d in range(n):
            g_qk[d, c] = part[d]
    deliver_qk = Deliver(table, 0, dqk, lambda d: g_qk.at[d], sem_c)
    part = t_dot(a, low_ref[2]).reshape(n, 2, rows, wide).astype(bf16)
    for d in range(n):
        for s in range(2):
            g_vo[d, s] = part[d, s]
    deliver_vo = Deliver(table, 1, dvo, lambda d: g_vo.at[d], sem_d)
    fetch_qk.wait()
    first = dot_t(low_ref[0], qk_weight(wqk, 0)) + dot_t(low_ref[1], qk_weight(wqk, 1))
    pfirst_out[...] = (first + dot_t(low_ref[2], v_weight(wvo))).astype(bf16)
    deliver_qk.wait()
    deliver_vo.wait()


VM = pl.BlockSpec(memory_space=pltpu.VMEM)
SM = pl.BlockSpec(memory_space=pltpu.SMEM)
ANY = pl.BlockSpec(memory_space=pl.ANY)


def shaped(shape, kind):
    return jax.ShapeDtypeStruct(shape, kind)


def launch(kernel, name, args, outs, scratch):
    call = pl.pallas_call(
        kernel,
        name=name,
        in_specs=[spec for _, spec in args],
        out_specs=[spec for _, _, spec in outs],
        out_shape=[shaped(shape, kind) for shape, kind, _ in outs],
        scratch_shapes=scratch,
    )
    return list(call(*[array for array, _ in args]))


def bound(function, *fixed):
    def kernel(*refs):
        function(*fixed, *refs)

    return kernel


def body(tokens, cotangent, lengths, owners, w_qkv, bias_qv, w_out, w_up, bias_up, w_down, vectors):
    size = lax.axis_size("dp")
    mover = Mover(size)
    capacity, width = tokens.shape
    wide = w_qkv.shape[-1]
    hidden_units = w_up.shape[-1]
    layers = w_qkv.shape[0]
    lined = mover.lined
    blocks = size if lined else 1
    parts = 2 if lined else 1
    per = blocks // parts

    small_parts = [
        vectors.reshape(layers, -1), bias_qv.reshape(layers, -1), bias_up.reshape(layers, -1)
    ]
    small_sizes = [part.shape[1] for part in small_parts]
    small = jnp.concatenate(small_parts, axis=1).reshape(-1)
    count = small.shape[0]
    padded = -(-count // 1024) * 1024
    small_block = jnp.pad(small, (0, padded - count)).reshape(-1, 128)

    def fetch(block, half):
        return mover.gather(block, half)

    small_halves = fetch(small_block, 0)
    packed = []
    for layer in range(layers):
        packed.append(pack_attention(w_qkv[layer], w_out[layer, 0]) + (w_up[layer], w_down[layer, 0]))
    gathered = [[fetch(packed[l][k], k % 2) for k in range(4)] for l in range(layers)]

    small_all = mover.absolute(jnp.concatenate(small_halves), 0).reshape(size, -1)[:, :count]
    small_all = small_all.reshape(size, layers, -1).astype(f32)
    edge = [0]
    for length in small_sizes:
        edge.append(edge[-1] + length)

    def spread(k, rows):
        piece = small_all[:, :, edge[k] : edge[k + 1]].reshape(size, layers, rows, -1)
        return piece.transpose(1, 2, 0, 3).reshape(layers, rows, -1)

    vec = spread(0, vectors.shape[1])
    bqv = spread(1, 2)
    bup = spread(2, 1)

    if lined:
        table = jnp.stack(mover.tables)
    else:
        table = jnp.zeros((2, 1), jnp.int32)

    def natural(k, halves):
        if lined:
            return list(halves)
        value = mover.absolute(jnp.concatenate(halves), k % 2)
        if k == 0:
            value = value.transpose(1, 0, 2, 3).reshape(1, 2, width, wide)
        elif k == 1:
            v = value[:, :2].reshape(2, wide, wide)
            o = value[:, 2:].transpose(1, 0, 2, 3).reshape(2, wide, wide)
            value = jnp.concatenate([v, o])[None]
        else:
            value = value.reshape(1, -1, value.shape[-1])
        return [value]

    weights = [[natural(k, gathered[l][k]) for k in range(4)] for l in range(layers)]
    shapes = [
        (blocks, 2, width // blocks, wide),
        (blocks, 4, wide // blocks, wide),
        (blocks, width // blocks, hidden_units),
        (blocks, hidden_units // blocks, width),
    ]
    part_shapes = [(per,) + shape[1:] for shape in shapes]

    segment_ids = slot_segments(lengths, owners, mover.me, capacity)
    live = (segment_ids < lengths.shape[0]).astype(f32)[:, None]
    seg_col, seg_row = segment_ids[:, None], segment_ids[None, :]

    def dma(n):
        return pltpu.SemaphoreType.DMA((n,))

    def holds(ks, grads=False):
        found = [pltpu.VMEM(shapes[k], bf16) for k in ks]
        if grads:
            found = found + found
        return found

    def swap(value):
        return lax.ppermute(value, "tensor", [(0, 1), (1, 0)])

    act = (capacity, width)
    tab = [(table, SM)]

    def vm(*arrays):
        return [(array, VM) for array in arrays]

    def hb(*lists):
        return [(array, ANY) for arrays in lists for array in arrays]

    def grad_outs(*ks):
        return [(part_shapes[k], bf16, ANY) for k in ks for _ in range(parts)]

    def attention_forward(layer, inputs):
        outs = [
            (act, bf16, VM),
            ((3, capacity, wide), bf16, VM),
            ((capacity, wide), bf16, VM),
            (act, f32, VM),
        ]
        if layer:
            outs = [(act, f32, VM)] + outs
        return launch(
            bound(attention_forward_kernel, layer, parts),
            "attention_forward",
            tab + vm(*inputs, vec[layer], bqv[layer], seg_col, seg_row)
            + hb(weights[layer][0], weights[layer][1]),
            outs,
            holds((0, 1)) + [dma(blocks), dma(blocks)],
        )

    normed0, qkv0, attended0, own = attention_forward(0, (tokens,))
    other = swap(own)
    middle0, second0, active0, own = launch(
        bound(ffn_forward_kernel, parts),
        "ffn_forward",
        tab + vm(tokens, own, other, vec[0], bup[0]) + hb(weights[0][2], weights[0][3]),
        [
            (act, f32, VM),
            (act, bf16, VM),
            ((capacity, hidden_units), bf16, VM),
            (act, f32, VM),
        ],
        holds((2, 3)) + [dma(blocks), dma(blocks)],
    )
    other = swap(own)
    hidden1, normed1, qkv1, attended1, own = attention_forward(1, (middle0, own, other, vec[0]))
    other = swap(own)

    outs = launch(
        bound(ffn_turn_kernel, parts),
        "ffn_turn",
        tab + vm(hidden1, own, other, vec[1], bup[1], cotangent, live)
        + hb(weights[1][2], weights[1][3]),
        [
            (act, f32, VM),
            (act, f32, VM),
            (act, bf16, VM),
            ((1, hidden_units), f32, VM),
            ((1, width), f32, VM),
        ]
        + grad_outs(2, 3),
        holds((2, 3), True) + [dma(blocks) for _ in range(4)],
    )
    middle1, down_own, psec, dbup1, dshift1 = outs[:5]
    dup1, ddown1 = outs[5 : 5 + parts], outs[5 + parts :]
    psec_other = swap(psec)
    down_other = swap(down_own)

    def attention_backward(layer, inputs, psec, psec_other, middle, attended, qkv, normed):
        outs = launch(
            bound(attention_backward_kernel, layer, parts),
            "attention_backward",
            tab
            + vm(*inputs, psec, psec_other, middle, vec[layer], attended, qkv, normed)
            + vm(seg_col, seg_row)
            + hb(weights[layer][0], weights[layer][1]),
            [
                (act, f32, VM),
                (act, bf16, VM),
                ((2, wide), f32, VM),
                ((3, width), f32, VM),
            ]
            + grad_outs(0, 1),
            holds((0, 1), True)
            + [pltpu.VMEM((3, capacity, wide), bf16)]
            + [dma(blocks) for _ in range(4)],
        )
        return outs[:4] + [outs[4 : 4 + parts], outs[4 + parts :]]

    mgrad1, pfirst, dbqv1, dmid1, dqk1, dvo1 = attention_backward(
        1, (cotangent, live), psec, psec_other, middle1, attended1, qkv1, normed1
    )
    pfirst_other = swap(pfirst)
    outs = launch(
        bound(ffn_backward_kernel, parts),
        "ffn_backward",
        tab + vm(mgrad1, pfirst, pfirst_other, hidden1, vec[1], second0, active0)
        + hb(weights[0][2], weights[0][3]),
        [
            (act, f32, VM),
            (act, bf16, VM),
            ((1, hidden_units), f32, VM),
            ((1, width), f32, VM),
            ((2, width), f32, VM),
        ]
        + grad_outs(2, 3),
        holds((2, 3), True) + [dma(blocks) for _ in range(4)],
    )
    g0, psec, dbup0, dshift0, dnorm1 = outs[:5]
    dup0, ddown0 = outs[5 : 5 + parts], outs[5 + parts :]
    psec_other = swap(psec)
    mgrad0, pfirst, dbqv0, dmid0, dqk0, dvo0 = attention_backward(
        0, (g0,), psec, psec_other, middle0, attended0, qkv0, normed0
    )
    pfirst_other = swap(pfirst)
    tokens_grad, dnorm0 = launch(
        last_kernel,
        "last",
        vm(mgrad0, pfirst, pfirst_other, tokens, vec[0]),
        [(act, f32, VM), ((2, width), f32, VM)],
        [],
    )

    def ordered(k, grads):
        if lined:
            return grads
        value = grads[0]
        if k == 0:
            value = value.reshape(2, size, -1, wide).transpose(1, 0, 2, 3)
        elif k == 1:
            v = value[0, :2].reshape(size, 2, -1, wide)
            o = value[0, 2:].reshape(2, size, -1, wide).transpose(1, 0, 2, 3)
            value = jnp.concatenate([v, o], axis=1)
        else:
            value = value.reshape(size, -1, value.shape[-1])
        value = jnp.take(value, mover.tables[k % 2], axis=0)
        return value[: size // 2], value[size // 2 :]

    def summed(k, grads):
        kept, sent = ordered(k, grads)
        return mover.reduce(kept, sent, k % 2)

    up1, down1 = summed(2, dup1), summed(3, ddown1)
    qk1, vo1 = summed(0, dqk1), summed(1, dvo1)
    up0, down0 = summed(2, dup0), summed(3, ddown0)
    qk0, vo0 = summed(0, dqk0), summed(1, dvo0)

    dvec = jnp.stack(
        [
            jnp.concatenate([dnorm0, dmid0, dshift0]),
            jnp.concatenate([dnorm1, dmid1, dshift1]),
        ]
    )
    dbqv = jnp.stack([dbqv0, dbqv1])
    dbup = jnp.stack([dbup0, dbup1])

    def shard(value):
        rows = value.shape[1]
        value = value.reshape(layers, rows, size, -1).transpose(2, 0, 1, 3)
        return value.reshape(size, layers, -1)

    small_grad = jnp.concatenate([shard(dvec), shard(dbqv), shard(dbup)], axis=2)
    small_grad = small_grad.reshape(size, -1)
    small_grad = jnp.pad(small_grad, ((0, 0), (0, padded - count))).reshape(size, -1, 128)
    small_grad = jnp.take(small_grad, mover.tables[0], axis=0)
    half = size // 2
    small_sum = mover.reduce(small_grad[:half], small_grad[half:], 0, f32).reshape(-1)[:count]
    small_sum = small_sum.reshape(layers, -1)
    vec_sum, bqv_sum, bup_sum = (small_sum[:, edge[k] : edge[k + 1]] for k in range(3))

    qkv_grad0, out_grad0 = unpack_attention(qk0, vo0)
    qkv_grad1, out_grad1 = unpack_attention(qk1, vo1)
    output = middle1 + ((down_own + down_other) + vec[1, 5:6])
    return (
        output,
        tokens_grad,
        jnp.stack([qkv_grad0, qkv_grad1]),
        bqv_sum.reshape(bias_qv.shape),
        jnp.stack([out_grad0, out_grad1]).reshape(w_out.shape),
        jnp.stack([up0, up1]),
        bup_sum.reshape(bias_up.shape),
        jnp.stack([down0, down1]).reshape(w_down.shape),
        vec_sum.reshape(vectors.shape),
    )


def solution(mesh):
    return jax.shard_map(
        body,
        mesh=mesh,
        in_specs=(
            P("dp", None),
            P("dp", None),
            P(),
            P(),
            P(None, None, "dp", "tensor"),
            P(None, None, "tensor", "dp"),
            P(None, "tensor", "dp", None),
            P(None, "dp", "tensor"),
            P(None, "tensor", "dp"),
            P(None, "tensor", "dp", None),
            P(None, None, "dp"),
        ),
        out_specs=(
            P("dp", None),
            P("dp", None),
            P(None, None, "dp", "tensor"),
            P(None, None, "tensor", "dp"),
            P(None, "tensor", "dp", None),
            P(None, "dp", "tensor"),
            P(None, "tensor", "dp"),
            P(None, "tensor", "dp", None),
            P(None, None, "dp"),
        ),
        check_vma=False,
    )
```

```python
import jax
import jax.numpy as jnp
from jax import lax
from jax.experimental import pallas as pl
from jax.experimental.pallas import tpu as pltpu
from jax.sharding import PartitionSpec as P


HD = 64
epsilon = 1e-05
masked_score = -1e30
bf16 = jnp.bfloat16
f32 = jnp.float32


GATHERS = (
    (((0, 0),), (8, 4, 1, 2)),
    (((1, 0),), (8, 1, 4, 2)),
    (((2, 0),), (8, 4, 2, 1)),
    (((3, 0),), (8, 1, 2, 4)),
    (((0, 1),), (8, 4, 1, 2)),
    (((1, 1),), (2, 8, 4, 1)),
    (((2, 1),), (8, 4, 2, 1)),
    (((3, 1),), (8, 2, 1, 4)),
)
REDUCTIONS = (
    ((2, 1), (8, 4, 1, 2)),
    ((3, 1), (8, 2, 1, 4)),
    ((0, 1), (8, 4, 2, 1)),
    ((1, 1), (8, 2, 1, 4)),
    ((2, 0), (8, 1, 2, 4)),
    ((3, 0), (8, 4, 1, 2)),
    ((0, 0), (8, 4, 1, 2)),
    ((1, 0), (8, 4, 1, 2)),
)


def slot_segments(lengths, owners, device, capacity):
    is_mine = owners == device
    owned_sizes = jnp.where(is_mine, lengths, 0)
    count = lengths.shape[0]
    order = jnp.arange(count, dtype=jnp.int32)
    before = order[None, :] < order[:, None]
    slot_begin = jnp.sum(jnp.where(before, owned_sizes[None, :], 0), axis=1)
    slot_ids = jnp.arange(capacity, dtype=jnp.int32)
    slot_end = slot_begin + owned_sizes
    inside = (
        is_mine[None, :]
        & (slot_ids[:, None] >= slot_begin[None, :])
        & (slot_ids[:, None] < slot_end[None, :])
    )
    matched = jnp.sum(jnp.where(inside, order[None, :] + 1, 0), axis=1)
    return jnp.where(matched > 0, matched - 1, count + slot_ids)


class Mover:
    def __init__(self, size, orders):
        self.size = size
        self.me = lax.axis_index("dp")
        self.orders = orders
        self.tables = [self.table(order) for order in orders]

    def swap(self, value, bit):
        return lax.ppermute(value, "dp", [(i, i ^ bit) for i in range(self.size)])

    def table(self, order):
        spots = self.me[None]
        for bit in order:
            spots = jnp.concatenate([spots, spots ^ bit])
        return spots.astype(jnp.int32)

    def gather(self, block, order):
        held = block[None]
        bits = self.orders[order]
        for bit in bits[:-1]:
            came = self.swap(held, bit)
            held = jnp.concatenate([held, came])
        return held, self.swap(held, bits[-1])

    def reduce(self, pair, order):
        bits = self.orders[order][::-1]
        own, came = pair[0], self.swap(pair[1], bits[0])
        for bit in bits[1:]:
            middle = own.shape[0] // 2
            out = (own[middle:].astype(f32) + came[middle:].astype(f32)).astype(bf16)
            own = own[:middle].astype(f32) + came[:middle].astype(f32)
            came = self.swap(out, bit)
        return (own + came.astype(f32))[0]

    def everywhere(self, value, bits):
        for bit in bits:
            came = self.swap(value, bit)
            value = value + came
        return value

    def absolute(self, blocks, order):
        devices = jnp.arange(self.size, dtype=jnp.int32)
        spots = self.tables[order]
        found = jnp.where(spots[None, :] == devices[:, None], devices[None, :], 0)
        return jnp.take(blocks, jnp.sum(found, axis=1), axis=0)


def beside(value):
    rows = value.shape[-2] // 2
    return jnp.concatenate([value[..., :rows, :], value[..., rows:, :]], axis=-1)


def below(value):
    wide = value.shape[-1] // 2
    return jnp.concatenate([value[..., :wide], value[..., wide:]], axis=-2)


def dot(a, b):
    return lax.dot_general(a, b, (((1,), (0,)), ((), ())), preferred_element_type=f32)


def dot_t(a, b):
    return lax.dot_general(a, b, (((1,), (1,)), ((), ())), preferred_element_type=f32)


def t_dot(a, b):
    return lax.dot_general(a, b, (((0,), (0,)), ((), ())), preferred_element_type=f32)


def norm_parts(hidden):
    mean_row = jnp.mean(hidden, axis=-1, keepdims=True)
    centered = hidden - mean_row
    inverse = lax.rsqrt(jnp.mean(centered * centered, axis=-1, keepdims=True) + epsilon)
    return centered * inverse, inverse


def norm_backward(incoming, hat, inverse, gain_row):
    gain_grad = jnp.sum(incoming * hat, axis=0, keepdims=True)
    shift_grad = jnp.sum(incoming, axis=0, keepdims=True)
    scaled = incoming * gain_row
    back = inverse * (
        scaled
        - jnp.mean(scaled, axis=-1, keepdims=True)
        - hat * jnp.mean(scaled * hat, axis=-1, keepdims=True)
    )
    return back, gain_grad, shift_grad


class Copies:
    def __init__(self, table, row, parts, pieces, sems, out=False):
        self.copies = []
        spot = 0
        for part in parts:
            for k in range(part.shape[0]):
                device = table[row, spot]
                for j, (begin, rows, place) in enumerate(pieces):
                    ends = part.at[k, pl.ds(begin, rows)], place(device)
                    if out:
                        ends = ends[::-1]
                    sem = sems.at[spot * len(pieces) + j]
                    self.copies.append(pltpu.make_async_copy(*ends, sem))
                spot += 1
        for copy in self.copies:
            copy.start()

    def wait(self):
        for copy in self.copies:
            copy.wait()


def whole_pieces(ref, begin=0):
    return [(begin, ref.shape[1], lambda d: ref.at[d])]


def half_pieces(ref, begin=0):
    rows = ref.shape[2]
    return [(begin + c * rows, rows, lambda d, c=c: ref.at[c, d]) for c in (0, 1)]


def attention_fetch(table, orders, qk, vo, begins, wqk, wvo, sem_a, sem_b):
    first = Copies(table, orders[0], qk, whole_pieces(wqk, begins[0]), sem_a)
    second = Copies(table, orders[1], vo, whole_pieces(wvo, begins[1]), sem_b)
    return first, second


class Small:
    def __init__(self, ref, layer, layers):
        self.ref, self.layer, self.layers = ref, layer, layers

    def at(self, spot):
        return self.ref[spot : spot + 1, :]

    def vec(self, k):
        return self.at(6 * self.layer + k)

    def bias_qv(self, c):
        row = self.at(6 * self.layers + self.layer)
        wide = row.shape[1] // 2
        return row[:, c * wide : (c + 1) * wide]

    def bias_up(self):
        spot = 7 * self.layers + 2 * self.layer
        return jnp.concatenate([self.at(spot), self.at(spot + 1)], axis=1)


def vo_weights(wvo):
    v, o = [], []
    for d in range(wvo.shape[0]):
        block = wvo[d].astype(f32)
        rows, wide = block.shape[0] // 2, block.shape[1] // 2
        v += [block[:rows, :wide], block[:rows, wide:]]
        o.append(block[rows:])
    return (jnp.concatenate(piece, axis=0).astype(bf16) for piece in (v, o))


def merged(ref, *lead):
    value = ref[lead] if lead else ref[...]
    return value.reshape(value.shape[0] * value.shape[1], value.shape[2])


def head_scores(q_pair, k_pair, mine, allowed):
    scores = dot_t(jnp.where(mine, q_pair, jnp.zeros_like(q_pair)), k_pair) * HD ** (-0.5)
    scores = jnp.where(allowed, scores, masked_score)
    row_max = jnp.max(scores, axis=-1, keepdims=True)
    lse = row_max + jnp.log(jnp.sum(jnp.exp(scores - row_max), axis=-1, keepdims=True))
    return jnp.exp(scores - lse)


def allowed_pairs(seg_col, seg_row):
    size = seg_col.shape[0]
    rows = lax.broadcasted_iota(jnp.int32, (size, size), 0)
    columns = lax.broadcasted_iota(jnp.int32, (size, size), 1)
    return (seg_col[...] == seg_row[...]) & (columns <= rows)


def lane_half(size):
    return lax.broadcasted_iota(jnp.int32, (size, 2 * HD), 1) < HD


def attention_forward_kernel(layer, layers, parts, orders, begins, *refs):
    refs = list(refs)
    take = lambda n: [refs.pop(0) for _ in range(n)]
    (table,) = take(1)
    if layer == 0:
        (tokens,) = take(1)
    else:
        middle, own, other = take(3)
    small, seg_col, seg_row = take(3)
    rows = Small(small, layer, layers)
    qk, vo = take(parts), take(parts)
    if layer:
        (hidden_out,) = take(1)
    normed_out, qkv_out, attended_out, partial_out = take(4)
    wqk, wvo, sem_a, sem_b = take(4)
    fetch_qk, fetch_vo = attention_fetch(
        table, orders, qk, vo, begins, wqk, wvo, sem_a, sem_b
    )
    if layer == 0:
        hidden = tokens[...].astype(f32)
    else:
        hidden = middle[...] + (
            (own[...] + other[...]) + Small(small, layer - 1, layers).vec(5)
        )
        hidden_out[...] = hidden
    hat, _ = norm_parts(hidden)
    normed = (hat * rows.vec(0) + rows.vec(1)).astype(bf16)
    normed_out[...] = normed
    allowed = allowed_pairs(seg_col, seg_row)
    low = lane_half(normed.shape[0])
    wide = attended_out.shape[1]
    fetch_qk.wait()
    both = dot(normed, merged(wqk))
    qkv_out[0] = (both[:, :wide] + rows.bias_qv(0)).astype(bf16)
    qkv_out[1] = both[:, wide:].astype(bf16)
    fetch_vo.wait()
    v_weight, o_weight = vo_weights(wvo)
    qkv_out[2] = (dot(normed, v_weight) + rows.bias_qv(1)).astype(bf16)
    for pair in range(wide // (2 * HD)):
        lanes = slice(pair * 2 * HD, (pair + 1) * 2 * HD)
        q, k, v = (qkv_out[c, :, lanes] for c in range(3))
        outs = []
        for mine in (low, ~low):
            probs = head_scores(q, k, mine, allowed)
            outs.append(dot(probs.astype(bf16), v))
        attended_out[:, lanes] = jnp.where(low, outs[0], outs[1]).astype(bf16)
    partial_out[...] = dot(attended_out[...], o_weight)


def feed_forward(hidden, own, other, rows, wup):
    middle = hidden + ((own + other) + rows.vec(2))
    hat, _ = norm_parts(middle)
    second = (hat * rows.vec(3) + rows.vec(4)).astype(bf16)
    before = jnp.concatenate([dot(second, merged(wup, c)) for c in (0, 1)], axis=1)
    active = jnp.maximum(before + rows.bias_up(), 0.0).astype(bf16)
    return middle, second, active


def feed_backward(
    gb, second, active, wup, wdown, g_up, g_down, outs, table, orders, sems
):
    psec_out, dup, ddown, dbias_out = outs
    act_grad = dot_t(gb, wdown)
    pre_grad = jnp.where(active > 0, act_grad, 0.0)
    pre_low = pre_grad.astype(bf16)
    g_down[...] = t_dot(active, gb).astype(bf16).reshape(g_down.shape)
    deliver_down = Copies(table, orders[3], ddown, whole_pieces(g_down), sems[1], True)
    wide = pre_low.shape[1] // 2
    back = 0.0
    for c in (0, 1):
        lanes = slice(c * wide, (c + 1) * wide)
        dbias_out[c : c + 1, :] = jnp.sum(pre_grad[:, lanes], axis=0, keepdims=True)
        low = pre_low[:, lanes]
        g_up[c] = t_dot(second, low).astype(bf16).reshape(g_up.shape[1:])
        back = back + dot_t(low, merged(wup, c))
    deliver_up = Copies(table, orders[2], dup, half_pieces(g_up), sems[0], True)
    psec_out[...] = back.astype(bf16)
    return deliver_up, deliver_down


def up_down_fetch(table, orders, up, down, begins, wup, wdown, sem_a, sem_b):
    first = Copies(table, orders[0], up, half_pieces(wup, begins[0]), sem_a)
    return first, Copies(table, orders[1], down, whole_pieces(wdown, begins[1]), sem_b)


def ffn_forward_kernel(
    layer, layers, parts, orders, begins, table, hidden, own, other, small, *refs
):
    refs = list(refs)
    take = lambda n: [refs.pop(0) for _ in range(n)]
    up, down = take(parts), take(parts)
    middle_out, second_out, active_out, partial_out = take(4)
    wup, wdown, sem_a, sem_b = take(4)
    fetch_up, fetch_down = up_down_fetch(
        table, orders, up, down, begins, wup, wdown, sem_a, sem_b
    )
    fetch_up.wait()
    middle, second, active = feed_forward(
        hidden[...].astype(f32), own[...], other[...], Small(small, layer, layers), wup
    )
    middle_out[...] = middle
    second_out[...] = second
    active_out[...] = active
    fetch_down.wait()
    partial_out[...] = dot(active, merged(wdown))


def ffn_turn_kernel(
    layer, layers, parts, orders, begins, table, hidden, own, other, small, cotangent, live,
    *refs,
):
    refs = list(refs)
    take = lambda n: [refs.pop(0) for _ in range(n)]
    up, down = take(parts), take(parts)
    middle_out, partial_out, psec_out, dbias_out, dshift_out = take(5)
    dup, ddown = take(parts), take(parts)
    wup, wdown, g_up, g_down, sem_a, sem_b, sem_c, sem_d = take(8)
    fetch_up, fetch_down = up_down_fetch(
        table, orders, up, down, begins, wup, wdown, sem_a, sem_b
    )
    g = cotangent[...].astype(f32) * live[...]
    dshift_out[...] = jnp.sum(g, axis=0, keepdims=True)
    fetch_up.wait()
    middle, second, active = feed_forward(
        hidden[...].astype(f32), own[...], other[...], Small(small, layer, layers), wup
    )
    middle_out[...] = middle
    fetch_down.wait()
    down_all = merged(wdown)
    delivered = feed_backward(
        g.astype(bf16), second, active, wup, down_all, g_up, g_down,
        (psec_out, dup, ddown, dbias_out), table, orders, (sem_c, sem_d),
    )
    partial_out[...] = dot(active, down_all)
    for one in delivered:
        one.wait()


def ffn_backward_kernel(
    layer, layers, parts, orders, begins, table, middle_grad, own, other, hidden, small, second,
    active, *refs,
):
    refs = list(refs)
    take = lambda n: [refs.pop(0) for _ in range(n)]
    up, down = take(parts), take(parts)
    g_out, psec_out, dbias_out, dshift_out, dnorm_out = take(5)
    dup, ddown = take(parts), take(parts)
    wup, wdown, g_up, g_down, sem_a, sem_b, sem_c, sem_d = take(8)
    fetch_up, fetch_down = up_down_fetch(
        table, orders, up, down, begins, wup, wdown, sem_a, sem_b
    )
    gain = Small(small, layer + 1, layers).vec(0)
    g = input_gradient(middle_grad, own, other, hidden, gain, dnorm_out)
    g_out[...] = g
    dshift_out[...] = jnp.sum(g, axis=0, keepdims=True)
    fetch_down.wait()
    fetch_up.wait()
    delivered = feed_backward(
        g.astype(bf16), second[...], active[...], wup, merged(wdown), g_up, g_down,
        (psec_out, dup, ddown, dbias_out), table, orders, (sem_c, sem_d),
    )
    for one in delivered:
        one.wait()


def input_gradient(middle_grad, own, other, hidden, gain, dnorm_out):
    first_grad = own[...].astype(f32) + other[...].astype(f32)
    hat, inverse = norm_parts(hidden[...].astype(f32))
    back, gain_grad, shift_grad = norm_backward(first_grad, hat, inverse, gain)
    dnorm_out[0:1, :] = gain_grad
    dnorm_out[1:2, :] = shift_grad
    return middle_grad[...] + back


def last_kernel(middle_grad, own, other, hidden, small, grad_out, dnorm_out):
    gain = small[0:1, :]
    grad_out[...] = input_gradient(middle_grad, own, other, hidden, gain, dnorm_out)


def attention_backward_kernel(layer, layers, parts, orders, begins, *refs):
    refs = list(refs)
    take = lambda n: [refs.pop(0) for _ in range(n)]
    (table,) = take(1)
    if layer:
        cotangent, live = take(2)
    else:
        (g_in,) = take(1)
    own, other, middle, small, attended_in, qkv, normed, seg_col, seg_row = take(9)
    gain = Small(small, layer, layers).vec(3)
    qk, vo = take(parts), take(parts)
    middle_grad_out, pfirst_out, dbias_out, dnorm_out = take(4)
    dqk, dvo = take(parts), take(parts)
    wqk, wvo, g_qk, g_vo, low_ref, sem_a, sem_b, sem_c, sem_d = take(9)
    fetch_qk, fetch_vo = attention_fetch(
        table, orders, qk, vo, begins, wqk, wvo, sem_a, sem_b
    )
    if layer:
        g = cotangent[...].astype(f32) * live[...]
    else:
        g = g_in[...]
    second_grad = own[...].astype(f32) + other[...].astype(f32)
    hat, inverse = norm_parts(middle[...])
    back, gain_grad, shift_grad = norm_backward(second_grad, hat, inverse, gain)
    middle_grad = g + back
    middle_grad_out[...] = middle_grad
    dnorm_out[0:1, :] = jnp.sum(middle_grad, axis=0, keepdims=True)
    dnorm_out[1:2, :] = gain_grad
    dnorm_out[2:3, :] = shift_grad
    middle_low = middle_grad.astype(bf16)
    allowed = allowed_pairs(seg_col, seg_row)
    low = lane_half(middle_low.shape[0])
    n, rows = g_vo.shape[:2]
    wide = g_vo.shape[2] // 2
    fetch_vo.wait()
    v_weight, o_weight = vo_weights(wvo)
    attended_grad = dot_t(middle_low, o_weight).astype(bf16)
    scale = HD ** (-0.5)
    for pair in range(wide // (2 * HD)):
        lanes = slice(pair * 2 * HD, (pair + 1) * 2 * HD)
        q, k, v = (qkv[c, :, lanes] for c in range(3))
        da = attended_grad[:, lanes]
        dq, dk, dv = [], [], []
        for mine in (low, ~low):
            probs = head_scores(q, k, mine, allowed)
            dv.append(t_dot(probs.astype(bf16), da))
            dprob = dot_t(jnp.where(mine, da, jnp.zeros_like(da)), v)
            row_dot = jnp.sum(probs * dprob, axis=-1, keepdims=True)
            ds = (probs * (dprob - row_dot) * scale).astype(bf16)
            dq.append(dot(ds, k))
            dk.append(t_dot(ds, q))
        dq = jnp.where(low, dq[0], dq[1])
        dk = jnp.where(low, dk[0], dk[1])
        dv = jnp.where(low, dv[0], dv[1])
        shifted = slice(lanes.start + wide, lanes.stop + wide)
        dbias_out[0:1, lanes] = jnp.sum(dq, axis=0, keepdims=True)
        dbias_out[0:1, shifted] = jnp.sum(dv, axis=0, keepdims=True)
        low_ref[0, :, lanes] = dq.astype(bf16)
        low_ref[0, :, shifted] = dk.astype(bf16)
        low_ref[1, :, lanes] = dv.astype(bf16)
    a = normed[...]
    dqk_low, dv_low = low_ref[0], low_ref[1, :, :wide]
    g_qk[...] = t_dot(a, dqk_low).astype(bf16).reshape(g_qk.shape)
    deliver_qk = Copies(table, orders[2], dqk, whole_pieces(g_qk), sem_c, True)
    o_grad = t_dot(attended_in[...], middle_low).reshape(n, rows // 2, 2 * wide)
    v_grad = t_dot(a, dv_low).reshape(n, 2, rows // 2, wide)
    for d in range(n):
        top = jnp.concatenate([v_grad[d, 0], v_grad[d, 1]], axis=1)
        g_vo[d] = jnp.concatenate([top, o_grad[d]], axis=0).astype(bf16)
    deliver_vo = Copies(table, orders[3], dvo, whole_pieces(g_vo), sem_d, True)
    fetch_qk.wait()
    first = dot_t(dqk_low, merged(wqk)) + dot_t(dv_low, v_weight)
    pfirst_out[...] = first.astype(bf16)
    deliver_qk.wait()
    deliver_vo.wait()


VM = pl.BlockSpec(memory_space=pltpu.VMEM)
SM = pl.BlockSpec(memory_space=pltpu.SMEM)
ANY = pl.BlockSpec(memory_space=pl.ANY)


def shaped(shape, kind):
    return jax.ShapeDtypeStruct(shape, kind)


def launch(kernel, args, outs, scratch):
    call = pl.pallas_call(
        kernel,
        in_specs=[spec for _, spec in args],
        out_specs=[spec for _, _, spec in outs],
        out_shape=[shaped(shape, kind) for shape, kind, _ in outs],
        scratch_shapes=scratch,
    )
    return list(call(*[array for array, _ in args]))


def bound(function, *fixed):
    def kernel(*refs):
        function(*fixed, *refs)

    return kernel


def whole_step(
    tokens, cotangent, lengths, owners, w_qkv, bias_qv, w_out, w_up, bias_up, w_down, vectors
):
    size = lax.axis_size("dp")
    capacity, width = tokens.shape
    wide = w_qkv.shape[-1]
    hidden_units = w_up.shape[-1]
    layers = w_qkv.shape[0]
    rows = width // size
    lined = size == 16
    blocks = size if lined else 1
    parts = 2 if lined else 1
    per = blocks // parts
    far_first = tuple(1 << k for k in range(size.bit_length() - 1))[::-1]
    gathers = GATHERS if lined else [(members, far_first) for members, _ in GATHERS]
    reductions = REDUCTIONS if lined else [(member, far_first) for member, _ in REDUCTIONS]
    orders = sorted({order for _, order in (*gathers, *reductions)})
    mover = Mover(size, orders)

    def placed(value, count):
        value = jnp.tile(value.reshape(count, -1), (1, size))
        owner = jnp.arange(value.shape[1], dtype=jnp.int32) // (value.shape[1] // size)
        return jnp.where(owner == mover.me, value, jnp.zeros_like(value)).reshape(-1, width)

    small = jnp.concatenate(
        [
            placed(vectors, layers * vectors.shape[1]),
            placed(bias_qv, 2 * layers),
            placed(bias_up, layers),
        ]
    )
    used = small.shape[0]
    tall = -(-used // 8) * 8
    small = jnp.pad(small, ((0, tall - used), (0, 0)))

    qk = [jnp.concatenate([w_qkv[l, 0], w_qkv[l, 1]], axis=1) for l in range(layers)]
    vo = [jnp.concatenate([beside(w_qkv[l, 2]), w_out[l, 0]]) for l in range(layers)]
    up = [below(w_up[l]) for l in range(layers)]
    down = [w_down[l, 0] for l in range(layers)]
    own_blocks = (qk, vo, up, down)

    places = {}
    for members, bits in gathers:
        pieces = [own_blocks[k][layer] for k, layer in members]
        block = pieces[0] if len(pieces) == 1 else jnp.concatenate(pieces)
        order = orders.index(bits)
        pair = mover.gather(block, order)
        begin = 0
        for member, piece in zip(members, pieces):
            places[member] = (pair, order, begin)
            begin += piece.shape[0]
    small = mover.everywhere(small, far_first).astype(f32)

    if lined:
        table = jnp.stack(mover.tables)
    else:
        table = jnp.zeros((1, 1), jnp.int32)

    def natural(k, pair, order, begin):
        if lined:
            return list(pair), begin, order
        many = rows if k < 2 else 2 * rows
        value = jnp.concatenate([part[:, begin : begin + many] for part in pair])
        value = mover.absolute(value, order)
        if k == 1:
            v = below(value[:, : rows // 2]).reshape(width, wide)
            value = jnp.concatenate([beside(v), value[:, rows // 2 :].reshape(wide, width)])
        elif k == 2:
            value = value.reshape(size, 2, rows, width).transpose(1, 0, 2, 3)
        return [value.reshape(1, -1, width)], 0, 0

    weights = [[natural(k, *places[k, l]) for k in range(4)] for l in range(layers)]
    reduced = {
        member: (number, orders.index(bits)) for number, (member, bits) in enumerate(reductions)
    }
    part_shapes = [(per, (1 + k // 2) * (width // blocks), width) for k in range(4)]
    shapes = [
        (blocks, width // blocks, width),
        (blocks, width // blocks, width),
        (2, blocks, width // blocks, width),
        (blocks, 2 * (width // blocks), width),
    ]

    segment_ids = slot_segments(lengths, owners, mover.me, capacity)
    live = (segment_ids < lengths.shape[0]).astype(f32)[:, None]
    seg_col, seg_row = segment_ids[:, None], segment_ids[None, :]

    def sems(*ks):
        return [pltpu.SemaphoreType.DMA(((1 + (k == 2)) * blocks,)) for k in ks]

    def holds(*ks):
        return [pltpu.VMEM(shapes[k], bf16) for k in ks]

    def swap(value):
        return lax.ppermute(value, "tensor", [(0, 1), (1, 0)])

    act = (capacity, width)
    tab = [(table, SM)]

    def vm(*arrays):
        return [(array, VM) for array in arrays]

    def hb(layer, *ks):
        return [(array, ANY) for k in ks for array in weights[layer][k][0]]

    def fixed(layer, *ks):
        fetched = tuple(weights[layer][k][2] for k in ks)
        sent = tuple(reduced[k, layer][1] if lined else 0 for k in ks)
        return layer, layers, parts, fetched + sent, tuple(weights[layer][k][1] for k in ks)

    def grad_outs(*ks):
        return [(part_shapes[k], bf16, ANY) for k in ks for _ in range(parts)]

    def attention_forward(layer, inputs):
        outs = [
            (act, bf16, VM),
            ((3, capacity, wide), bf16, VM),
            ((capacity, wide), bf16, VM),
            (act, f32, VM),
        ]
        if layer:
            outs = [(act, f32, VM)] + outs
        return launch(
            bound(attention_forward_kernel, *fixed(layer, 0, 1)),
            tab + vm(*inputs, small, seg_col, seg_row) + hb(layer, 0, 1),
            outs,
            holds(0, 1) + sems(0, 1),
        )

    normed0, qkv0, attended0, own = attention_forward(0, (tokens,))
    other = swap(own)
    middle0, second0, active0, own = launch(
        bound(ffn_forward_kernel, *fixed(0, 2, 3)),
        tab + vm(tokens, own, other, small) + hb(0, 2, 3),
        [
            (act, f32, VM),
            (act, bf16, VM),
            ((capacity, hidden_units), bf16, VM),
            (act, f32, VM),
        ],
        holds(2, 3) + sems(2, 3),
    )
    other = swap(own)
    hidden1, normed1, qkv1, attended1, own = attention_forward(1, (middle0, own, other))
    other = swap(own)

    outs = launch(
        bound(ffn_turn_kernel, *fixed(1, 2, 3)),
        tab + vm(hidden1, own, other, small, cotangent, live) + hb(1, 2, 3),
        [
            (act, f32, VM),
            (act, f32, VM),
            (act, bf16, VM),
            ((hidden_units // width, width), f32, VM),
            ((1, width), f32, VM),
        ]
        + grad_outs(2, 3),
        holds(2, 3, 2, 3) + sems(2, 3, 2, 3),
    )
    middle1, down_own, psec, dbup1, dshift1 = outs[:5]
    dup1, ddown1 = outs[5 : 5 + parts], outs[5 + parts :]

    def summed(k, layer, grads):
        _, order = reduced[k, layer]
        if lined:
            return mover.reduce(grads, order)
        value = grads[0][0]
        if k == 1:
            v = below(value[:wide]).reshape(size, rows, wide)
            value = jnp.concatenate([beside(v), value[wide:].reshape(size, -1, width)], axis=1)
        elif k == 2:
            value = value.reshape(2, size, rows, width).transpose(1, 0, 2, 3)
        value = jnp.take(value.reshape(size, -1, width), mover.tables[order], axis=0)
        return mover.reduce((value[: size // 2], value[size // 2 :]), order)

    up1, down1 = summed(2, 1, dup1), summed(3, 1, ddown1)
    psec_other = swap(psec)
    down_other = swap(down_own)

    def attention_backward(layer, inputs, psec, psec_other, middle, attended, qkv, normed):
        outs = launch(
            bound(attention_backward_kernel, *fixed(layer, 0, 1)),
            tab
            + vm(*inputs, psec, psec_other, middle, small, attended, qkv, normed)
            + vm(seg_col, seg_row)
            + hb(layer, 0, 1),
            [
                (act, f32, VM),
                (act, bf16, VM),
                ((1, width), f32, VM),
                ((3, width), f32, VM),
            ]
            + grad_outs(0, 1),
            holds(0, 1, 0, 1)
            + [pltpu.VMEM((2, capacity, width), bf16)]
            + sems(0, 1, 0, 1),
        )
        return outs[:4] + [outs[4 : 4 + parts], outs[4 + parts :]]

    mgrad1, pfirst, dbqv1, dmid1, dqk1, dvo1 = attention_backward(
        1, (cotangent, live), psec, psec_other, middle1, attended1, qkv1, normed1
    )
    qk1, vo1 = summed(0, 1, dqk1), summed(1, 1, dvo1)
    pfirst_other = swap(pfirst)
    outs = launch(
        bound(ffn_backward_kernel, *fixed(0, 2, 3)),
        tab + vm(mgrad1, pfirst, pfirst_other, hidden1, small, second0, active0)
        + hb(0, 2, 3),
        [
            (act, f32, VM),
            (act, bf16, VM),
            ((hidden_units // width, width), f32, VM),
            ((1, width), f32, VM),
            ((2, width), f32, VM),
        ]
        + grad_outs(2, 3),
        holds(2, 3, 2, 3) + sems(2, 3, 2, 3),
    )
    g0, psec, dbup0, dshift0, dnorm1 = outs[:5]
    dup0, ddown0 = outs[5 : 5 + parts], outs[5 + parts :]
    up0, down0 = summed(2, 0, dup0), summed(3, 0, ddown0)
    psec_other = swap(psec)
    mgrad0, pfirst, dbqv0, dmid0, dqk0, dvo0 = attention_backward(
        0, (g0,), psec, psec_other, middle0, attended0, qkv0, normed0
    )
    qk0, vo0 = summed(0, 0, dqk0), summed(1, 0, dvo0)
    pfirst_other = swap(pfirst)
    tokens_grad, dnorm0 = launch(
        last_kernel,
        vm(mgrad0, pfirst, pfirst_other, tokens, small),
        [(act, f32, VM), ((2, width), f32, VM)],
        [],
    )

    small_grad = jnp.concatenate(
        [dnorm0, dmid0, dshift0, dnorm1, dmid1, dshift1, dbqv0, dbqv1, dbup0, dbup1]
    )
    small_grad = jnp.pad(small_grad, ((0, tall - used), (0, 0)))
    small_sum = mover.everywhere(small_grad, far_first[::-1])

    def mine(begin, end, count):
        value = small_sum[begin:end].reshape(count, -1)
        many = value.shape[1] // size
        return lax.dynamic_slice(value, (0, mover.me * many), (count, many))

    six = vectors.shape[1] * layers
    vec_sum = mine(0, six, six)
    bqv_sum = mine(six, six + layers, 2 * layers)
    bup_sum = mine(six + layers, used, layers)

    def qkv_of(qk_sum, vo_sum):
        v = below(vo_sum[: rows // 2])
        return jnp.stack([qk_sum[:, :wide], qk_sum[:, wide:], v])

    output = middle1 + ((down_own + down_other) + small[six - 1 : six])
    return (
        output,
        tokens_grad,
        jnp.stack([qkv_of(qk0, vo0), qkv_of(qk1, vo1)]),
        bqv_sum.reshape(bias_qv.shape),
        jnp.stack([vo0[rows // 2 :], vo1[rows // 2 :]]).reshape(w_out.shape),
        jnp.stack([beside(up0), beside(up1)]),
        bup_sum.reshape(bias_up.shape),
        jnp.stack([down0, down1]).reshape(w_down.shape),
        vec_sum.reshape(vectors.shape),
    )


def solution(mesh):
    return sharded(mesh)


def sharded(mesh):
    return jax.shard_map(
        whole_step,
        mesh=mesh,
        in_specs=(
            P("dp", None),
            P("dp", None),
            P(),
            P(),
            P(None, None, "dp", "tensor"),
            P(None, None, "tensor", "dp"),
            P(None, "tensor", "dp", None),
            P(None, "dp", "tensor"),
            P(None, "tensor", "dp"),
            P(None, "tensor", "dp", None),
            P(None, None, "dp"),
        ),
        out_specs=(
            P("dp", None),
            P("dp", None),
            P(None, None, "dp", "tensor"),
            P(None, None, "tensor", "dp"),
            P(None, "tensor", "dp", None),
            P(None, "dp", "tensor"),
            P(None, "tensor", "dp"),
            P(None, "tensor", "dp", None),
            P(None, None, "dp"),
        ),
        check_vma=False,
    )
```

```python
import jax
import jax.numpy as jnp
from jax import lax
from jax.experimental import pallas as pl
from jax.experimental.pallas import tpu as pltpu
from jax.sharding import PartitionSpec as P


HD = 64
epsilon = 1e-05
masked_score = -1e30
bf16 = jnp.bfloat16
f32 = jnp.float32


GATHERS = (
    (((0, 0),), (8, 4, 1, 2)),
    (((1, 0),), (8, 4, 2, 1)),
    (((2, 0),), (8, 2, 4, 1)),
    (((3, 0),), (8, 2, 1, 4)),
    (((0, 1), (1, 1),), (8, 1, 4, 2)),
    (((2, 1),), (8, 1, 2, 4)),
    (((3, 1),), (8, 4, 2, 1)),
)
REDUCTIONS = (
    (((2, 1),), (8, 4, 2, 1)),
    (((3, 1),), (8, 1, 2, 4)),
    (((0, 1), (1, 1),), (8, 4, 1, 2)),
    (((2, 0),), (8, 4, 2, 1)),
    (((3, 0),), (8, 2, 1, 4)),
    (((0, 0),), (8, 4, 2, 1)),
    (((1, 0),), (8, 2, 1, 4)),
)


def slot_segments(lengths, owners, device, capacity):
    is_mine = owners == device
    owned_sizes = jnp.where(is_mine, lengths, 0)
    count = lengths.shape[0]
    order = jnp.arange(count, dtype=jnp.int32)
    before = order[None, :] < order[:, None]
    slot_begin = jnp.sum(jnp.where(before, owned_sizes[None, :], 0), axis=1)
    slot_ids = jnp.arange(capacity, dtype=jnp.int32)
    slot_end = slot_begin + owned_sizes
    inside = (
        is_mine[None, :]
        & (slot_ids[:, None] >= slot_begin[None, :])
        & (slot_ids[:, None] < slot_end[None, :])
    )
    matched = jnp.sum(jnp.where(inside, order[None, :] + 1, 0), axis=1)
    return jnp.where(matched > 0, matched - 1, count + slot_ids)


class Mover:
    def __init__(self, size, orders):
        self.size = size
        self.me = lax.axis_index("dp")
        self.orders = orders
        self.tables = [self.table(order) for order in orders]

    def swap(self, value, bit):
        return lax.ppermute(value, "dp", [(i, i ^ bit) for i in range(self.size)])

    def table(self, order):
        spots = self.me[None]
        for bit in order:
            spots = jnp.concatenate([spots, spots ^ bit])
        return spots.astype(jnp.int32)

    def gather(self, block, order):
        held = block[None]
        bits = self.orders[order]
        for bit in bits[:-1]:
            came = self.swap(held, bit)
            held = jnp.concatenate([held, came])
        return held, self.swap(held, bits[-1])

    def reduce(self, pair, order):
        bits = self.orders[order][::-1]
        own, came = pair[0], self.swap(pair[1], bits[0])
        for bit in bits[1:]:
            middle = own.shape[0] // 2
            out = (own[middle:].astype(f32) + came[middle:].astype(f32)).astype(bf16)
            own = own[:middle].astype(f32) + came[:middle].astype(f32)
            came = self.swap(out, bit)
        return (own + came.astype(f32))[0]

    def everywhere(self, value, bits):
        for bit in bits:
            came = self.swap(value, bit)
            value = value + came
        return value

    def absolute(self, blocks, order):
        devices = jnp.arange(self.size, dtype=jnp.int32)
        spots = self.tables[order]
        found = jnp.where(spots[None, :] == devices[:, None], devices[None, :], 0)
        return jnp.take(blocks, jnp.sum(found, axis=1), axis=0)


def beside(value):
    rows = value.shape[-2] // 2
    return jnp.concatenate([value[..., :rows, :], value[..., rows:, :]], axis=-1)


def below(value):
    wide = value.shape[-1] // 2
    return jnp.concatenate([value[..., :wide], value[..., wide:]], axis=-2)


def dot(a, b):
    return lax.dot_general(a, b, (((1,), (0,)), ((), ())), preferred_element_type=f32)


def dot_t(a, b):
    return lax.dot_general(a, b, (((1,), (1,)), ((), ())), preferred_element_type=f32)


def t_dot(a, b):
    return lax.dot_general(a, b, (((0,), (0,)), ((), ())), preferred_element_type=f32)


def norm_parts(hidden):
    mean_row = jnp.mean(hidden, axis=-1, keepdims=True)
    centered = hidden - mean_row
    inverse = lax.rsqrt(jnp.mean(centered * centered, axis=-1, keepdims=True) + epsilon)
    return centered * inverse, inverse


def norm_backward(incoming, hat, inverse, gain_row):
    gain_grad = jnp.sum(incoming * hat, axis=0, keepdims=True)
    shift_grad = jnp.sum(incoming, axis=0, keepdims=True)
    scaled = incoming * gain_row
    back = inverse * (
        scaled
        - jnp.mean(scaled, axis=-1, keepdims=True)
        - hat * jnp.mean(scaled * hat, axis=-1, keepdims=True)
    )
    return back, gain_grad, shift_grad


class Copies:
    def __init__(self, table, row, parts, pieces, sems, out=False):
        self.copies = []
        spot = 0
        for part in parts:
            for k in range(part.shape[0]):
                device = table[row, spot]
                for j, (begin, rows, place) in enumerate(pieces):
                    ends = part.at[k, pl.ds(begin, rows)], place(device)
                    if out:
                        ends = ends[::-1]
                    sem = sems.at[spot * len(pieces) + j]
                    self.copies.append(pltpu.make_async_copy(*ends, sem))
                spot += 1
        for copy in self.copies:
            copy.start()

    def wait(self):
        for copy in self.copies:
            copy.wait()


def whole_pieces(ref, begin=0):
    return [(begin, ref.shape[1], lambda d: ref.at[d])]


def half_pieces(ref, begin=0):
    rows = ref.shape[2]
    return [(begin + c * rows, rows, lambda d, c=c: ref.at[c, d]) for c in (0, 1)]


def attention_fetch(table, orders, qk, vo, begins, wqk, wvo, sem_a, sem_b):
    first = Copies(table, orders[0], qk, whole_pieces(wqk, begins[0]), sem_a)
    second = Copies(table, orders[1], vo, whole_pieces(wvo, begins[1]), sem_b)
    return first, second


class Small:
    def __init__(self, ref, layer, layers):
        self.ref, self.layer, self.layers = ref, layer, layers

    def at(self, spot):
        return self.ref[spot : spot + 1, :]

    def vec(self, k):
        return self.at(6 * self.layer + k)

    def bias_qv(self, c):
        row = self.at(6 * self.layers + self.layer)
        wide = row.shape[1] // 2
        return row[:, c * wide : (c + 1) * wide]

    def bias_up(self):
        spot = 7 * self.layers + 2 * self.layer
        return jnp.concatenate([self.at(spot), self.at(spot + 1)], axis=1)


def vo_weights(wvo):
    v, o = [], []
    for d in range(wvo.shape[0]):
        block = wvo[d].astype(f32)
        rows, wide = block.shape[0] // 2, block.shape[1] // 2
        v += [block[:rows, :wide], block[:rows, wide:]]
        o.append(block[rows:])
    return (jnp.concatenate(piece, axis=0).astype(bf16) for piece in (v, o))


def merged(ref, *lead):
    value = ref[lead] if lead else ref[...]
    return value.reshape(value.shape[0] * value.shape[1], value.shape[2])


def head_scores(q_pair, k_pair, mine, allowed):
    scores = dot_t(jnp.where(mine, q_pair, jnp.zeros_like(q_pair)), k_pair) * HD ** (-0.5)
    scores = jnp.where(allowed, scores, masked_score)
    row_max = jnp.max(scores, axis=-1, keepdims=True)
    lse = row_max + jnp.log(jnp.sum(jnp.exp(scores - row_max), axis=-1, keepdims=True))
    return jnp.exp(scores - lse)


def allowed_pairs(seg_col, seg_row):
    size = seg_col.shape[0]
    rows = lax.broadcasted_iota(jnp.int32, (size, size), 0)
    columns = lax.broadcasted_iota(jnp.int32, (size, size), 1)
    return (seg_col[...] == seg_row[...]) & (columns <= rows)


def lane_half(size):
    return lax.broadcasted_iota(jnp.int32, (size, 2 * HD), 1) < HD


def attention_forward_kernel(layer, layers, parts, orders, begins, *refs):
    refs = list(refs)
    take = lambda n: [refs.pop(0) for _ in range(n)]
    (table,) = take(1)
    if layer == 0:
        (tokens,) = take(1)
    else:
        middle, own, other = take(3)
    small, seg_col, seg_row = take(3)
    rows = Small(small, layer, layers)
    qk, vo = take(parts), take(parts)
    if layer:
        (hidden_out,) = take(1)
    normed_out, qkv_out, attended_out, partial_out = take(4)
    wqk, wvo, sem_a, sem_b = take(4)
    fetch_qk, fetch_vo = attention_fetch(
        table, orders, qk, vo, begins, wqk, wvo, sem_a, sem_b
    )
    if layer == 0:
        hidden = tokens[...].astype(f32)
    else:
        hidden = middle[...] + (
            (own[...] + other[...]) + Small(small, layer - 1, layers).vec(5)
        )
        hidden_out[...] = hidden
    hat, _ = norm_parts(hidden)
    normed = (hat * rows.vec(0) + rows.vec(1)).astype(bf16)
    normed_out[...] = normed
    allowed = allowed_pairs(seg_col, seg_row)
    low = lane_half(normed.shape[0])
    wide = attended_out.shape[1]
    fetch_qk.wait()
    both = dot(normed, merged(wqk))
    qkv_out[0] = (both[:, :wide] + rows.bias_qv(0)).astype(bf16)
    qkv_out[1] = both[:, wide:].astype(bf16)
    fetch_vo.wait()
    v_weight, o_weight = vo_weights(wvo)
    qkv_out[2] = (dot(normed, v_weight) + rows.bias_qv(1)).astype(bf16)
    for pair in range(wide // (2 * HD)):
        lanes = slice(pair * 2 * HD, (pair + 1) * 2 * HD)
        q, k, v = (qkv_out[c, :, lanes] for c in range(3))
        outs = []
        for mine in (low, ~low):
            probs = head_scores(q, k, mine, allowed)
            outs.append(dot(probs.astype(bf16), v))
        attended_out[:, lanes] = jnp.where(low, outs[0], outs[1]).astype(bf16)
    partial_out[...] = dot(attended_out[...], o_weight)


def feed_forward(hidden, own, other, rows, wup):
    middle = hidden + ((own + other) + rows.vec(2))
    hat, _ = norm_parts(middle)
    second = (hat * rows.vec(3) + rows.vec(4)).astype(bf16)
    before = jnp.concatenate([dot(second, merged(wup, c)) for c in (0, 1)], axis=1)
    active = jnp.maximum(before + rows.bias_up(), 0.0).astype(bf16)
    return middle, second, active


def feed_backward(
    gb, second, active, wup, wdown, g_up, g_down, outs, table, orders, sems
):
    psec_out, dup, ddown, dbias_out = outs
    act_grad = dot_t(gb, wdown)
    pre_grad = jnp.where(active > 0, act_grad, 0.0)
    pre_low = pre_grad.astype(bf16)
    g_down[...] = t_dot(active, gb).astype(bf16).reshape(g_down.shape)
    deliver_down = Copies(table, orders[3], ddown, whole_pieces(g_down), sems[1], True)
    wide = pre_low.shape[1] // 2
    back = 0.0
    for c in (0, 1):
        lanes = slice(c * wide, (c + 1) * wide)
        dbias_out[c : c + 1, :] = jnp.sum(pre_grad[:, lanes], axis=0, keepdims=True)
        low = pre_low[:, lanes]
        g_up[c] = t_dot(second, low).astype(bf16).reshape(g_up.shape[1:])
        back = back + dot_t(low, merged(wup, c))
    deliver_up = Copies(table, orders[2], dup, half_pieces(g_up), sems[0], True)
    psec_out[...] = back.astype(bf16)
    return deliver_up, deliver_down


def up_down_fetch(table, orders, up, down, begins, wup, wdown, sem_a, sem_b):
    first = Copies(table, orders[0], up, half_pieces(wup, begins[0]), sem_a)
    return first, Copies(table, orders[1], down, whole_pieces(wdown, begins[1]), sem_b)


def ffn_forward_kernel(
    layer, layers, parts, orders, begins, table, hidden, own, other, small, *refs
):
    refs = list(refs)
    take = lambda n: [refs.pop(0) for _ in range(n)]
    up, down = take(parts), take(parts)
    middle_out, second_out, active_out, partial_out = take(4)
    wup, wdown, sem_a, sem_b = take(4)
    fetch_up, fetch_down = up_down_fetch(
        table, orders, up, down, begins, wup, wdown, sem_a, sem_b
    )
    fetch_up.wait()
    middle, second, active = feed_forward(
        hidden[...].astype(f32), own[...], other[...], Small(small, layer, layers), wup
    )
    middle_out[...] = middle
    second_out[...] = second
    active_out[...] = active
    fetch_down.wait()
    partial_out[...] = dot(active, merged(wdown))


def ffn_turn_kernel(
    layer, layers, parts, orders, begins, table, hidden, own, other, small, cotangent, live,
    *refs,
):
    refs = list(refs)
    take = lambda n: [refs.pop(0) for _ in range(n)]
    up, down = take(parts), take(parts)
    middle_out, partial_out, psec_out, dbias_out, dshift_out = take(5)
    dup, ddown = take(parts), take(parts)
    wup, wdown, g_up, g_down, sem_a, sem_b, sem_c, sem_d = take(8)
    fetch_up, fetch_down = up_down_fetch(
        table, orders, up, down, begins, wup, wdown, sem_a, sem_b
    )
    g = cotangent[...].astype(f32) * live[...]
    dshift_out[...] = jnp.sum(g, axis=0, keepdims=True)
    fetch_up.wait()
    middle, second, active = feed_forward(
        hidden[...].astype(f32), own[...], other[...], Small(small, layer, layers), wup
    )
    middle_out[...] = middle
    fetch_down.wait()
    down_all = merged(wdown)
    delivered = feed_backward(
        g.astype(bf16), second, active, wup, down_all, g_up, g_down,
        (psec_out, dup, ddown, dbias_out), table, orders, (sem_c, sem_d),
    )
    partial_out[...] = dot(active, down_all)
    for one in delivered:
        one.wait()


def ffn_backward_kernel(
    layer, layers, parts, orders, begins, table, middle_grad, own, other, hidden, small, second,
    active, *refs,
):
    refs = list(refs)
    take = lambda n: [refs.pop(0) for _ in range(n)]
    up, down = take(parts), take(parts)
    g_out, psec_out, dbias_out, dshift_out, dnorm_out = take(5)
    dup, ddown = take(parts), take(parts)
    wup, wdown, g_up, g_down, sem_a, sem_b, sem_c, sem_d = take(8)
    fetch_up, fetch_down = up_down_fetch(
        table, orders, up, down, begins, wup, wdown, sem_a, sem_b
    )
    gain = Small(small, layer + 1, layers).vec(0)
    g = input_gradient(middle_grad, own, other, hidden, gain, dnorm_out)
    g_out[...] = g
    dshift_out[...] = jnp.sum(g, axis=0, keepdims=True)
    fetch_down.wait()
    fetch_up.wait()
    delivered = feed_backward(
        g.astype(bf16), second[...], active[...], wup, merged(wdown), g_up, g_down,
        (psec_out, dup, ddown, dbias_out), table, orders, (sem_c, sem_d),
    )
    for one in delivered:
        one.wait()


def input_gradient(middle_grad, own, other, hidden, gain, dnorm_out):
    first_grad = own[...].astype(f32) + other[...].astype(f32)
    hat, inverse = norm_parts(hidden[...].astype(f32))
    back, gain_grad, shift_grad = norm_backward(first_grad, hat, inverse, gain)
    dnorm_out[0:1, :] = gain_grad
    dnorm_out[1:2, :] = shift_grad
    return middle_grad[...] + back


def last_kernel(middle_grad, own, other, hidden, small, grad_out, dnorm_out):
    gain = small[0:1, :]
    grad_out[...] = input_gradient(middle_grad, own, other, hidden, gain, dnorm_out)


def attention_backward_kernel(apart, g_rows, layer, layers, parts, orders, begins, *refs):
    refs = list(refs)
    take = lambda n: [refs.pop(0) for _ in range(n)]
    (table,) = take(1)
    if layer:
        cotangent, live = take(2)
    else:
        (g_in,) = take(1)
    own, other, middle, small, attended_in, qkv, normed, seg_col, seg_row = take(9)
    gain = Small(small, layer, layers).vec(3)
    qk, vo = take(parts), take(parts)
    middle_grad_out, pfirst_out, dbias_out, dnorm_out = take(4)
    dqk = take(parts)
    dvo, down_rows = (take(parts), 0) if apart else (dqk, g_rows)
    wqk, wvo, g_qk, g_vo, low_ref, sem_a, sem_b, sem_c, sem_d = take(9)
    fetch_qk, fetch_vo = attention_fetch(
        table, orders, qk, vo, begins, wqk, wvo, sem_a, sem_b
    )
    if layer:
        g = cotangent[...].astype(f32) * live[...]
    else:
        g = g_in[...]
    second_grad = own[...].astype(f32) + other[...].astype(f32)
    hat, inverse = norm_parts(middle[...])
    back, gain_grad, shift_grad = norm_backward(second_grad, hat, inverse, gain)
    middle_grad = g + back
    middle_grad_out[...] = middle_grad
    dnorm_out[0:1, :] = jnp.sum(middle_grad, axis=0, keepdims=True)
    dnorm_out[1:2, :] = gain_grad
    dnorm_out[2:3, :] = shift_grad
    middle_low = middle_grad.astype(bf16)
    allowed = allowed_pairs(seg_col, seg_row)
    low = lane_half(middle_low.shape[0])
    n, rows = g_vo.shape[:2]
    wide = g_vo.shape[2] // 2
    fetch_vo.wait()
    v_weight, o_weight = vo_weights(wvo)
    attended_grad = dot_t(middle_low, o_weight).astype(bf16)
    scale = HD ** (-0.5)
    for pair in range(wide // (2 * HD)):
        lanes = slice(pair * 2 * HD, (pair + 1) * 2 * HD)
        q, k, v = (qkv[c, :, lanes] for c in range(3))
        da = attended_grad[:, lanes]
        dq, dk, dv = [], [], []
        for mine in (low, ~low):
            probs = head_scores(q, k, mine, allowed)
            dv.append(t_dot(probs.astype(bf16), da))
            dprob = dot_t(jnp.where(mine, da, jnp.zeros_like(da)), v)
            row_dot = jnp.sum(probs * dprob, axis=-1, keepdims=True)
            ds = (probs * (dprob - row_dot) * scale).astype(bf16)
            dq.append(dot(ds, k))
            dk.append(t_dot(ds, q))
        dq = jnp.where(low, dq[0], dq[1])
        dk = jnp.where(low, dk[0], dk[1])
        dv = jnp.where(low, dv[0], dv[1])
        shifted = slice(lanes.start + wide, lanes.stop + wide)
        dbias_out[0:1, lanes] = jnp.sum(dq, axis=0, keepdims=True)
        dbias_out[0:1, shifted] = jnp.sum(dv, axis=0, keepdims=True)
        low_ref[0, :, lanes] = dq.astype(bf16)
        low_ref[0, :, shifted] = dk.astype(bf16)
        low_ref[1, :, lanes] = dv.astype(bf16)
    a = normed[...]
    dqk_low, dv_low = low_ref[0], low_ref[1, :, :wide]
    g_qk[...] = t_dot(a, dqk_low).astype(bf16).reshape(g_qk.shape)
    deliver_qk = Copies(table, orders[2], dqk, whole_pieces(g_qk), sem_c, True)
    o_grad = t_dot(attended_in[...], middle_low).reshape(n, rows // 2, 2 * wide)
    v_grad = t_dot(a, dv_low).reshape(n, 2, rows // 2, wide)
    for d in range(n):
        top = jnp.concatenate([v_grad[d, 0], v_grad[d, 1]], axis=1)
        g_vo[d] = jnp.concatenate([top, o_grad[d]], axis=0).astype(bf16)
    deliver_vo = Copies(table, orders[3], dvo, whole_pieces(g_vo, down_rows), sem_d, True)
    fetch_qk.wait()
    first = dot_t(dqk_low, merged(wqk)) + dot_t(dv_low, v_weight)
    pfirst_out[...] = first.astype(bf16)
    deliver_qk.wait()
    deliver_vo.wait()


VM = pl.BlockSpec(memory_space=pltpu.VMEM)
SM = pl.BlockSpec(memory_space=pltpu.SMEM)
ANY = pl.BlockSpec(memory_space=pl.ANY)


def shaped(shape, kind):
    return jax.ShapeDtypeStruct(shape, kind)


def launch(kernel, args, outs, scratch):
    call = pl.pallas_call(
        kernel,
        in_specs=[spec for _, spec in args],
        out_specs=[spec for _, _, spec in outs],
        out_shape=[shaped(shape, kind) for shape, kind, _ in outs],
        scratch_shapes=scratch,
    )
    return list(call(*[array for array, _ in args]))


def bound(function, *fixed):
    def kernel(*refs):
        function(*fixed, *refs)

    return kernel


def whole_step(
    tokens, cotangent, lengths, owners, w_qkv, bias_qv, w_out, w_up, bias_up, w_down, vectors
):
    size = lax.axis_size("dp")
    capacity, width = tokens.shape
    wide = w_qkv.shape[-1]
    hidden_units = w_up.shape[-1]
    layers = w_qkv.shape[0]
    rows = width // size
    lined = size == 16
    blocks = size if lined else 1
    parts = 2 if lined else 1
    per = blocks // parts
    far_first = tuple(1 << k for k in range(size.bit_length() - 1))[::-1]
    gathers = GATHERS if lined else [(members, far_first) for members, _ in GATHERS]
    reductions = REDUCTIONS
    if not lined:
        every = [member for members, _ in REDUCTIONS for member in members]
        reductions = [((member,), far_first) for member in every]
    orders = sorted({order for _, order in (*gathers, *reductions)})
    mover = Mover(size, orders)

    def placed(value, count):
        value = jnp.tile(value.reshape(count, -1), (1, size))
        owner = jnp.arange(value.shape[1], dtype=jnp.int32) // (value.shape[1] // size)
        return jnp.where(owner == mover.me, value, jnp.zeros_like(value)).reshape(-1, width)

    small = jnp.concatenate(
        [
            placed(vectors, layers * vectors.shape[1]),
            placed(bias_qv, 2 * layers),
            placed(bias_up, layers),
        ]
    )
    used = small.shape[0]
    tall = -(-used // 8) * 8
    small = jnp.pad(small, ((0, tall - used), (0, 0)))

    qk = [jnp.concatenate([w_qkv[l, 0], w_qkv[l, 1]], axis=1) for l in range(layers)]
    vo = [jnp.concatenate([beside(w_qkv[l, 2]), w_out[l, 0]]) for l in range(layers)]
    up = [below(w_up[l]) for l in range(layers)]
    down = [w_down[l, 0] for l in range(layers)]
    own_blocks = (qk, vo, up, down)

    places = {}
    for members, bits in gathers:
        pieces = [own_blocks[k][layer] for k, layer in members]
        block = pieces[0] if len(pieces) == 1 else jnp.concatenate(pieces)
        order = orders.index(bits)
        pair = mover.gather(block, order)
        begin = 0
        for member, piece in zip(members, pieces):
            places[member] = (pair, order, begin)
            begin += piece.shape[0]
    small = mover.everywhere(small, far_first).astype(f32)

    if lined:
        table = jnp.stack(mover.tables)
    else:
        table = jnp.zeros((1, 1), jnp.int32)

    def natural(k, pair, order, begin):
        if lined:
            return list(pair), begin, order
        many = rows if k < 2 else 2 * rows
        value = jnp.concatenate([part[:, begin : begin + many] for part in pair])
        value = mover.absolute(value, order)
        if k == 1:
            v = below(value[:, : rows // 2]).reshape(width, wide)
            value = jnp.concatenate([beside(v), value[:, rows // 2 :].reshape(wide, width)])
        elif k == 2:
            value = value.reshape(size, 2, rows, width).transpose(1, 0, 2, 3)
        return [value.reshape(1, -1, width)], 0, 0

    weights = [[natural(k, *places[k, l]) for k in range(4)] for l in range(layers)]
    reduced = {
        member: (number, orders.index(bits), len(members))
        for number, (members, bits) in enumerate(reductions)
        for member in members
    }
    part_shapes = [(per, (1 + k // 2) * (width // blocks), width) for k in range(4)]
    shapes = [
        (blocks, width // blocks, width),
        (blocks, width // blocks, width),
        (2, blocks, width // blocks, width),
        (blocks, 2 * (width // blocks), width),
    ]

    segment_ids = slot_segments(lengths, owners, mover.me, capacity)
    live = (segment_ids < lengths.shape[0]).astype(f32)[:, None]
    seg_col, seg_row = segment_ids[:, None], segment_ids[None, :]

    def sems(*ks):
        return [pltpu.SemaphoreType.DMA(((1 + (k == 2)) * blocks,)) for k in ks]

    def holds(*ks):
        return [pltpu.VMEM(shapes[k], bf16) for k in ks]

    def swap(value):
        return lax.ppermute(value, "tensor", [(0, 1), (1, 0)])

    act = (capacity, width)
    tab = [(table, SM)]

    def vm(*arrays):
        return [(array, VM) for array in arrays]

    def hb(layer, *ks):
        return [(array, ANY) for k in ks for array in weights[layer][k][0]]

    def fixed(layer, *ks):
        fetched = tuple(weights[layer][k][2] for k in ks)
        sent = tuple(reduced[k, layer][1] if lined else 0 for k in ks)
        return layer, layers, parts, fetched + sent, tuple(weights[layer][k][1] for k in ks)

    def grad_outs(*ks):
        return [(part_shapes[k], bf16, ANY) for k in ks for _ in range(parts)]

    def attention_forward(layer, inputs):
        outs = [
            (act, bf16, VM),
            ((3, capacity, wide), bf16, VM),
            ((capacity, wide), bf16, VM),
            (act, f32, VM),
        ]
        if layer:
            outs = [(act, f32, VM)] + outs
        return launch(
            bound(attention_forward_kernel, *fixed(layer, 0, 1)),
            tab + vm(*inputs, small, seg_col, seg_row) + hb(layer, 0, 1),
            outs,
            holds(0, 1) + sems(0, 1),
        )

    normed0, qkv0, attended0, own = attention_forward(0, (tokens,))
    other = swap(own)
    middle0, second0, active0, own = launch(
        bound(ffn_forward_kernel, *fixed(0, 2, 3)),
        tab + vm(tokens, own, other, small) + hb(0, 2, 3),
        [
            (act, f32, VM),
            (act, bf16, VM),
            ((capacity, hidden_units), bf16, VM),
            (act, f32, VM),
        ],
        holds(2, 3) + sems(2, 3),
    )
    other = swap(own)
    hidden1, normed1, qkv1, attended1, own = attention_forward(1, (middle0, own, other))
    other = swap(own)

    outs = launch(
        bound(ffn_turn_kernel, *fixed(1, 2, 3)),
        tab + vm(hidden1, own, other, small, cotangent, live) + hb(1, 2, 3),
        [
            (act, f32, VM),
            (act, f32, VM),
            (act, bf16, VM),
            ((hidden_units // width, width), f32, VM),
            ((1, width), f32, VM),
        ]
        + grad_outs(2, 3),
        holds(2, 3, 2, 3) + sems(2, 3, 2, 3),
    )
    middle1, down_own, psec, dbup1, dshift1 = outs[:5]
    dup1, ddown1 = outs[5 : 5 + parts], outs[5 + parts :]

    def summed(k, layer, grads):
        _, order, _ = reduced[k, layer]
        if lined:
            return mover.reduce(grads, order)
        value = grads[0][0]
        if k == 1:
            v = below(value[:wide]).reshape(size, rows, wide)
            value = jnp.concatenate([beside(v), value[wide:].reshape(size, -1, width)], axis=1)
        elif k == 2:
            value = value.reshape(2, size, rows, width).transpose(1, 0, 2, 3)
        value = jnp.take(value.reshape(size, -1, width), mover.tables[order], axis=0)
        return mover.reduce((value[: size // 2], value[size // 2 :]), order)

    def summed_attention(layer, dqk, dvo):
        first = summed(0, layer, dqk)
        if dvo:
            return first, summed(1, layer, dvo)
        return first[:rows], first[rows:]

    up1, down1 = summed(2, 1, dup1), summed(3, 1, ddown1)
    psec_other = swap(psec)
    down_other = swap(down_own)

    def attention_backward(layer, inputs, psec, psec_other, middle, attended, qkv, normed):
        apart = reduced[0, layer][2] == 1
        many = width // blocks
        sent = grad_outs(0, 1)
        if not apart:
            sent = [((per, 2 * many, width), bf16, ANY) for _ in range(parts)]
        outs = launch(
            bound(attention_backward_kernel, apart, many, *fixed(layer, 0, 1)),
            tab
            + vm(*inputs, psec, psec_other, middle, small, attended, qkv, normed)
            + vm(seg_col, seg_row)
            + hb(layer, 0, 1),
            [
                (act, f32, VM),
                (act, bf16, VM),
                ((1, width), f32, VM),
                ((3, width), f32, VM),
            ]
            + sent,
            holds(0, 1, 0, 1)
            + [pltpu.VMEM((2, capacity, width), bf16)]
            + sems(0, 1, 0, 1),
        )
        return outs[:4] + [outs[4 : 4 + parts], outs[4 + parts :]]

    mgrad1, pfirst, dbqv1, dmid1, dqk1, dvo1 = attention_backward(
        1, (cotangent, live), psec, psec_other, middle1, attended1, qkv1, normed1
    )
    qk1, vo1 = summed_attention(1, dqk1, dvo1)
    pfirst_other = swap(pfirst)
    outs = launch(
        bound(ffn_backward_kernel, *fixed(0, 2, 3)),
        tab + vm(mgrad1, pfirst, pfirst_other, hidden1, small, second0, active0)
        + hb(0, 2, 3),
        [
            (act, f32, VM),
            (act, bf16, VM),
            ((hidden_units // width, width), f32, VM),
            ((1, width), f32, VM),
            ((2, width), f32, VM),
        ]
        + grad_outs(2, 3),
        holds(2, 3, 2, 3) + sems(2, 3, 2, 3),
    )
    g0, psec, dbup0, dshift0, dnorm1 = outs[:5]
    dup0, ddown0 = outs[5 : 5 + parts], outs[5 + parts :]
    up0, down0 = summed(2, 0, dup0), summed(3, 0, ddown0)
    psec_other = swap(psec)
    mgrad0, pfirst, dbqv0, dmid0, dqk0, dvo0 = attention_backward(
        0, (g0,), psec, psec_other, middle0, attended0, qkv0, normed0
    )
    qk0, vo0 = summed_attention(0, dqk0, dvo0)
    pfirst_other = swap(pfirst)
    tokens_grad, dnorm0 = launch(
        last_kernel,
        vm(mgrad0, pfirst, pfirst_other, tokens, small),
        [(act, f32, VM), ((2, width), f32, VM)],
        [],
    )

    small_grad = jnp.concatenate(
        [dnorm0, dmid0, dshift0, dnorm1, dmid1, dshift1, dbqv0, dbqv1, dbup0, dbup1]
    )
    small_grad = jnp.pad(small_grad, ((0, tall - used), (0, 0)))
    small_sum = mover.everywhere(small_grad, far_first[::-1])

    def mine(begin, end, count):
        value = small_sum[begin:end].reshape(count, -1)
        many = value.shape[1] // size
        return lax.dynamic_slice(value, (0, mover.me * many), (count, many))

    six = vectors.shape[1] * layers
    vec_sum = mine(0, six, six)
    bqv_sum = mine(six, six + layers, 2 * layers)
    bup_sum = mine(six + layers, used, layers)

    def qkv_of(qk_sum, vo_sum):
        v = below(vo_sum[: rows // 2])
        return jnp.stack([qk_sum[:, :wide], qk_sum[:, wide:], v])

    output = middle1 + ((down_own + down_other) + small[six - 1 : six])
    return (
        output,
        tokens_grad,
        jnp.stack([qkv_of(qk0, vo0), qkv_of(qk1, vo1)]),
        bqv_sum.reshape(bias_qv.shape),
        jnp.stack([vo0[rows // 2 :], vo1[rows // 2 :]]).reshape(w_out.shape),
        jnp.stack([beside(up0), beside(up1)]),
        bup_sum.reshape(bias_up.shape),
        jnp.stack([down0, down1]).reshape(w_down.shape),
        vec_sum.reshape(vectors.shape),
    )


def solution(mesh):
    return sharded(mesh)


def sharded(mesh):
    return jax.shard_map(
        whole_step,
        mesh=mesh,
        in_specs=(
            P("dp", None),
            P("dp", None),
            P(),
            P(),
            P(None, None, "dp", "tensor"),
            P(None, None, "tensor", "dp"),
            P(None, "tensor", "dp", None),
            P(None, "dp", "tensor"),
            P(None, "tensor", "dp"),
            P(None, "tensor", "dp", None),
            P(None, None, "dp"),
        ),
        out_specs=(
            P("dp", None),
            P("dp", None),
            P(None, None, "dp", "tensor"),
            P(None, None, "tensor", "dp"),
            P(None, "tensor", "dp", None),
            P(None, "dp", "tensor"),
            P(None, "tensor", "dp"),
            P(None, "tensor", "dp", None),
            P(None, None, "dp"),
        ),
        check_vma=False,
    )
```

```python
import jax
import jax.numpy as jnp
from jax import lax
from jax.experimental import pallas as pl
from jax.experimental.pallas import tpu as pltpu
from jax.sharding import PartitionSpec as P


HD = 64
epsilon = 1e-05
masked_score = -1e30
bf16 = jnp.bfloat16
f32 = jnp.float32


GATHERS = (
    (((0, 0),), (8, 4, 1, 2)),
    (((1, 0),), (8, 4, 2, 1)),
    (((2, 0),), (8, 2, 4, 1)),
    (((3, 0),), (8, 2, 1, 4)),
    (((0, 1), (1, 1),), (8, 1, 4, 2)),
    (((2, 1),), (8, 1, 2, 4)),
    (((3, 1),), (8, 4, 2, 1)),
)
REDUCTIONS = (
    (((2, 1),), (8, 4, 2, 1)),
    (((3, 1),), (8, 1, 2, 4)),
    (((0, 1), (1, 1),), (8, 4, 1, 2)),
    (((2, 0),), (8, 4, 2, 1)),
    (((3, 0),), (8, 2, 1, 4)),
    (((0, 0),), (8, 4, 2, 1)),
    (((1, 0),), (8, 2, 1, 4)),
)


def slot_segments(lengths, owners, device, capacity):
    is_mine = owners == device
    owned_sizes = jnp.where(is_mine, lengths, 0)
    count = lengths.shape[0]
    order = jnp.arange(count, dtype=jnp.int32)
    before = order[None, :] < order[:, None]
    slot_begin = jnp.sum(jnp.where(before, owned_sizes[None, :], 0), axis=1)
    slot_ids = jnp.arange(capacity, dtype=jnp.int32)
    slot_end = slot_begin + owned_sizes
    inside = (
        is_mine[None, :]
        & (slot_ids[:, None] >= slot_begin[None, :])
        & (slot_ids[:, None] < slot_end[None, :])
    )
    matched = jnp.sum(jnp.where(inside, order[None, :] + 1, 0), axis=1)
    return jnp.where(matched > 0, matched - 1, count + slot_ids)


class Mover:
    def __init__(self, size, orders):
        self.size = size
        self.me = lax.axis_index("dp")
        self.orders = orders
        self.tables = [self.table(order) for order in orders]

    def swap(self, value, bit):
        return lax.ppermute(value, "dp", [(i, i ^ bit) for i in range(self.size)])

    def table(self, order):
        spots = self.me[None]
        for bit in order:
            spots = jnp.concatenate([spots, spots ^ bit])
        return spots.astype(jnp.int32)

    def gather(self, block, order):
        held = block[None]
        bits = self.orders[order]
        for bit in bits[:-1]:
            came = self.swap(held, bit)
            held = jnp.concatenate([held, came])
        return held, self.swap(held, bits[-1])

    def reduce(self, pair, order):
        bits = self.orders[order][::-1]
        own, came = pair[0], self.swap(pair[1], bits[0])
        for bit in bits[1:]:
            middle = own.shape[0] // 2
            out = (own[middle:].astype(f32) + came[middle:].astype(f32)).astype(bf16)
            own = own[:middle].astype(f32) + came[:middle].astype(f32)
            came = self.swap(out, bit)
        return (own + came.astype(f32))[0]

    def everywhere(self, value, bits):
        for bit in bits:
            came = self.swap(value, bit)
            value = value + came
        return value

    def absolute(self, blocks, order):
        devices = jnp.arange(self.size, dtype=jnp.int32)
        spots = self.tables[order]
        found = jnp.where(spots[None, :] == devices[:, None], devices[None, :], 0)
        return jnp.take(blocks, jnp.sum(found, axis=1), axis=0)


def beside(value):
    rows = value.shape[-2] // 2
    return jnp.concatenate([value[..., :rows, :], value[..., rows:, :]], axis=-1)


def below(value):
    wide = value.shape[-1] // 2
    return jnp.concatenate([value[..., :wide], value[..., wide:]], axis=-2)


def dot(a, b):
    return lax.dot_general(a, b, (((1,), (0,)), ((), ())), preferred_element_type=f32)


def dot_t(a, b):
    return lax.dot_general(a, b, (((1,), (1,)), ((), ())), preferred_element_type=f32)


def t_dot(a, b):
    return lax.dot_general(a, b, (((0,), (0,)), ((), ())), preferred_element_type=f32)


def norm_parts(hidden):
    mean_row = jnp.mean(hidden, axis=-1, keepdims=True)
    centered = hidden - mean_row
    inverse = lax.rsqrt(jnp.mean(centered * centered, axis=-1, keepdims=True) + epsilon)
    return centered * inverse, inverse


def norm_backward(incoming, hat, inverse, gain_row):
    gain_grad = jnp.sum(incoming * hat, axis=0, keepdims=True)
    shift_grad = jnp.sum(incoming, axis=0, keepdims=True)
    scaled = incoming * gain_row
    back = inverse * (
        scaled
        - jnp.mean(scaled, axis=-1, keepdims=True)
        - hat * jnp.mean(scaled * hat, axis=-1, keepdims=True)
    )
    return back, gain_grad, shift_grad


class Copies:
    def __init__(self, table, row, parts, pieces, sems, out=False):
        self.copies = []
        spot = 0
        for part in parts:
            for k in range(part.shape[0]):
                device = table[row, spot]
                for j, (begin, rows, place) in enumerate(pieces):
                    ends = part.at[k, pl.ds(begin, rows)], place(device)
                    if out:
                        ends = ends[::-1]
                    sem = sems.at[spot * len(pieces) + j]
                    self.copies.append(pltpu.make_async_copy(*ends, sem))
                spot += 1
        for copy in self.copies:
            copy.start()

    def wait(self):
        for copy in self.copies:
            copy.wait()


def whole_pieces(ref, begin=0):
    return [(begin, ref.shape[1], lambda d: ref.at[d])]


def half_pieces(ref, begin=0):
    rows = ref.shape[2]
    return [(begin + c * rows, rows, lambda d, c=c: ref.at[c, d]) for c in (0, 1)]


def attention_fetch(table, orders, qk, vo, begins, wqk, wvo, sem_a, sem_b):
    first = Copies(table, orders[0], qk, whole_pieces(wqk, begins[0]), sem_a)
    second = Copies(table, orders[1], vo, whole_pieces(wvo, begins[1]), sem_b)
    return first, second


class Small:
    def __init__(self, ref, layer, layers):
        self.ref, self.layer, self.layers = ref, layer, layers

    def at(self, spot):
        return self.ref[spot : spot + 1, :]

    def vec(self, k):
        return self.at(6 * self.layer + k)

    def bias_qv(self, c):
        row = self.at(6 * self.layers + self.layer)
        wide = row.shape[1] // 2
        return row[:, c * wide : (c + 1) * wide]

    def bias_up(self):
        spot = 7 * self.layers + 2 * self.layer
        return jnp.concatenate([self.at(spot), self.at(spot + 1)], axis=1)


def vo_weights(wvo):
    v, o = [], []
    for d in range(wvo.shape[0]):
        block = wvo[d].astype(f32)
        rows, wide = block.shape[0] // 2, block.shape[1] // 2
        v += [block[:rows, :wide], block[:rows, wide:]]
        o.append(block[rows:])
    return (jnp.concatenate(piece, axis=0).astype(bf16) for piece in (v, o))


def merged(ref, *lead):
    value = ref[lead] if lead else ref[...]
    return value.reshape(value.shape[0] * value.shape[1], value.shape[2])


def head_scores(q_pair, k_pair, mine, allowed):
    scores = dot_t(jnp.where(mine, q_pair, jnp.zeros_like(q_pair)), k_pair) * HD ** (-0.5)
    scores = jnp.where(allowed, scores, masked_score)
    row_max = jnp.max(scores, axis=-1, keepdims=True)
    lse = row_max + jnp.log(jnp.sum(jnp.exp(scores - row_max), axis=-1, keepdims=True))
    return jnp.exp(scores - lse)


def allowed_pairs(seg_col, seg_row):
    size = seg_col.shape[0]
    rows = lax.broadcasted_iota(jnp.int32, (size, size), 0)
    columns = lax.broadcasted_iota(jnp.int32, (size, size), 1)
    return (seg_col[...] == seg_row[...]) & (columns <= rows)


def lane_half(size):
    return lax.broadcasted_iota(jnp.int32, (size, 2 * HD), 1) < HD


def attention_forward_kernel(layer, layers, parts, orders, begins, *refs):
    refs = list(refs)
    take = lambda n: [refs.pop(0) for _ in range(n)]
    (table,) = take(1)
    if layer == 0:
        (tokens,) = take(1)
    else:
        middle, own, other = take(3)
    small, seg_col, seg_row = take(3)
    rows = Small(small, layer, layers)
    qk, vo = take(parts), take(parts)
    if layer:
        (hidden_out,) = take(1)
    normed_out, qkv_out, attended_out, partial_out = take(4)
    wqk, wvo, sem_a, sem_b = take(4)
    fetch_qk, fetch_vo = attention_fetch(
        table, orders, qk, vo, begins, wqk, wvo, sem_a, sem_b
    )
    if layer == 0:
        hidden = tokens[...].astype(f32)
    else:
        hidden = middle[...] + (
            (own[...] + other[...]) + Small(small, layer - 1, layers).vec(5)
        )
        hidden_out[...] = hidden
    hat, _ = norm_parts(hidden)
    normed = (hat * rows.vec(0) + rows.vec(1)).astype(bf16)
    normed_out[...] = normed
    allowed = allowed_pairs(seg_col, seg_row)
    low = lane_half(normed.shape[0])
    wide = attended_out.shape[1]
    fetch_qk.wait()
    both = dot(normed, merged(wqk))
    qkv_out[0] = (both[:, :wide] + rows.bias_qv(0)).astype(bf16)
    qkv_out[1] = both[:, wide:].astype(bf16)
    fetch_vo.wait()
    v_weight, o_weight = vo_weights(wvo)
    qkv_out[2] = (dot(normed, v_weight) + rows.bias_qv(1)).astype(bf16)
    for pair in range(wide // (2 * HD)):
        lanes = slice(pair * 2 * HD, (pair + 1) * 2 * HD)
        q, k, v = (qkv_out[c, :, lanes] for c in range(3))
        outs = []
        for mine in (low, ~low):
            probs = head_scores(q, k, mine, allowed)
            outs.append(dot(probs.astype(bf16), v))
        attended_out[:, lanes] = jnp.where(low, outs[0], outs[1]).astype(bf16)
    partial_out[...] = dot(attended_out[...], o_weight)


def feed_forward(hidden, own, other, rows, wup):
    middle = hidden + ((own + other) + rows.vec(2))
    hat, _ = norm_parts(middle)
    second = (hat * rows.vec(3) + rows.vec(4)).astype(bf16)
    before = jnp.concatenate([dot(second, merged(wup, c)) for c in (0, 1)], axis=1)
    active = jnp.maximum(before + rows.bias_up(), 0.0).astype(bf16)
    return middle, second, active


def feed_backward(
    gb, second, active, wup, wdown, g_up, g_down, outs, table, orders, sems
):
    psec_out, dup, ddown, dbias_out = outs
    act_grad = dot_t(gb, wdown)
    pre_grad = jnp.where(active > 0, act_grad, 0.0)
    pre_low = pre_grad.astype(bf16)
    g_down[...] = t_dot(active, gb).astype(bf16).reshape(g_down.shape)
    deliver_down = Copies(table, orders[3], ddown, whole_pieces(g_down), sems[1], True)
    wide = pre_low.shape[1] // 2
    blocks, rows = g_up.shape[1:3]
    lows, delivered = [], [deliver_down]
    for c in (0, 1):
        lanes = slice(c * wide, (c + 1) * wide)
        low = pre_low[:, lanes]
        g_up[c] = t_dot(second, low).astype(bf16).reshape(g_up.shape[1:])
        piece = [(c * rows, rows, lambda d, c=c: g_up.at[c, d])]
        some = sems[0].at[pl.ds(c * blocks, blocks)]
        delivered.append(Copies(table, orders[2], dup, piece, some, True))
        dbias_out[c : c + 1, :] = jnp.sum(pre_grad[:, lanes], axis=0, keepdims=True)
        lows.append(low)
    back = dot_t(lows[0], merged(wup, 0)) + dot_t(lows[1], merged(wup, 1))
    psec_out[...] = back.astype(bf16)
    return delivered


def up_down_fetch(table, orders, up, down, begins, wup, wdown, sem_a, sem_b):
    first = Copies(table, orders[0], up, half_pieces(wup, begins[0]), sem_a)
    return first, Copies(table, orders[1], down, whole_pieces(wdown, begins[1]), sem_b)


def ffn_forward_kernel(
    layer, layers, parts, orders, begins, table, hidden, own, other, small, *refs
):
    refs = list(refs)
    take = lambda n: [refs.pop(0) for _ in range(n)]
    up, down = take(parts), take(parts)
    middle_out, second_out, active_out, partial_out = take(4)
    wup, wdown, sem_a, sem_b = take(4)
    fetch_up, fetch_down = up_down_fetch(
        table, orders, up, down, begins, wup, wdown, sem_a, sem_b
    )
    fetch_up.wait()
    middle, second, active = feed_forward(
        hidden[...].astype(f32), own[...], other[...], Small(small, layer, layers), wup
    )
    middle_out[...] = middle
    second_out[...] = second
    active_out[...] = active
    fetch_down.wait()
    partial_out[...] = dot(active, merged(wdown))


def ffn_turn_kernel(
    layer, layers, parts, orders, begins, table, hidden, own, other, small, cotangent, live,
    *refs,
):
    refs = list(refs)
    take = lambda n: [refs.pop(0) for _ in range(n)]
    up, down = take(parts), take(parts)
    middle_out, partial_out, psec_out, dbias_out, dshift_out = take(5)
    dup, ddown = take(parts), take(parts)
    wup, wdown, g_up, g_down, sem_a, sem_b, sem_c, sem_d = take(8)
    fetch_up, fetch_down = up_down_fetch(
        table, orders, up, down, begins, wup, wdown, sem_a, sem_b
    )
    g = cotangent[...].astype(f32) * live[...]
    dshift_out[...] = jnp.sum(g, axis=0, keepdims=True)
    fetch_up.wait()
    middle, second, active = feed_forward(
        hidden[...].astype(f32), own[...], other[...], Small(small, layer, layers), wup
    )
    middle_out[...] = middle
    fetch_down.wait()
    down_all = merged(wdown)
    delivered = feed_backward(
        g.astype(bf16), second, active, wup, down_all, g_up, g_down,
        (psec_out, dup, ddown, dbias_out), table, orders, (sem_c, sem_d),
    )
    partial_out[...] = dot(active, down_all)
    for one in delivered:
        one.wait()


def ffn_backward_kernel(
    layer, layers, parts, orders, begins, table, middle_grad, own, other, hidden, small, second,
    active, *refs,
):
    refs = list(refs)
    take = lambda n: [refs.pop(0) for _ in range(n)]
    up, down = take(parts), take(parts)
    g_out, psec_out, dbias_out, dshift_out, dnorm_out = take(5)
    dup, ddown = take(parts), take(parts)
    wup, wdown, g_up, g_down, sem_a, sem_b, sem_c, sem_d = take(8)
    fetch_up, fetch_down = up_down_fetch(
        table, orders, up, down, begins, wup, wdown, sem_a, sem_b
    )
    gain = Small(small, layer + 1, layers).vec(0)
    g = input_gradient(middle_grad, own, other, hidden, gain, dnorm_out)
    g_out[...] = g
    dshift_out[...] = jnp.sum(g, axis=0, keepdims=True)
    fetch_down.wait()
    fetch_up.wait()
    delivered = feed_backward(
        g.astype(bf16), second[...], active[...], wup, merged(wdown), g_up, g_down,
        (psec_out, dup, ddown, dbias_out), table, orders, (sem_c, sem_d),
    )
    for one in delivered:
        one.wait()


def input_gradient(middle_grad, own, other, hidden, gain, dnorm_out):
    first_grad = own[...].astype(f32) + other[...].astype(f32)
    hat, inverse = norm_parts(hidden[...].astype(f32))
    back, gain_grad, shift_grad = norm_backward(first_grad, hat, inverse, gain)
    dnorm_out[0:1, :] = gain_grad
    dnorm_out[1:2, :] = shift_grad
    return middle_grad[...] + back


def last_kernel(middle_grad, own, other, hidden, small, grad_out, dnorm_out):
    gain = small[0:1, :]
    grad_out[...] = input_gradient(middle_grad, own, other, hidden, gain, dnorm_out)


def attention_backward_kernel(apart, g_rows, layer, layers, parts, orders, begins, *refs):
    refs = list(refs)
    take = lambda n: [refs.pop(0) for _ in range(n)]
    (table,) = take(1)
    if layer:
        cotangent, live = take(2)
    else:
        (g_in,) = take(1)
    own, other, middle, small, attended_in, qkv, normed, seg_col, seg_row = take(9)
    gain = Small(small, layer, layers).vec(3)
    qk, vo = take(parts), take(parts)
    middle_grad_out, pfirst_out, dbias_out, dnorm_out = take(4)
    dqk = take(parts)
    dvo, down_rows = (take(parts), 0) if apart else (dqk, g_rows)
    wqk, wvo, g_qk, g_vo, low_ref, sem_a, sem_b, sem_c, sem_d = take(9)
    fetch_qk, fetch_vo = attention_fetch(
        table, orders, qk, vo, begins, wqk, wvo, sem_a, sem_b
    )
    if layer:
        g = cotangent[...].astype(f32) * live[...]
    else:
        g = g_in[...]
    second_grad = own[...].astype(f32) + other[...].astype(f32)
    hat, inverse = norm_parts(middle[...])
    back, gain_grad, shift_grad = norm_backward(second_grad, hat, inverse, gain)
    middle_grad = g + back
    middle_grad_out[...] = middle_grad
    dnorm_out[0:1, :] = jnp.sum(middle_grad, axis=0, keepdims=True)
    dnorm_out[1:2, :] = gain_grad
    dnorm_out[2:3, :] = shift_grad
    middle_low = middle_grad.astype(bf16)
    allowed = allowed_pairs(seg_col, seg_row)
    low = lane_half(middle_low.shape[0])
    n, rows = g_vo.shape[:2]
    wide = g_vo.shape[2] // 2
    fetch_vo.wait()
    v_weight, o_weight = vo_weights(wvo)
    attended_grad = dot_t(middle_low, o_weight).astype(bf16)
    scale = HD ** (-0.5)
    for pair in range(wide // (2 * HD)):
        lanes = slice(pair * 2 * HD, (pair + 1) * 2 * HD)
        q, k, v = (qkv[c, :, lanes] for c in range(3))
        da = attended_grad[:, lanes]
        dq, dk, dv = [], [], []
        for mine in (low, ~low):
            probs = head_scores(q, k, mine, allowed)
            dv.append(t_dot(probs.astype(bf16), da))
            dprob = dot_t(jnp.where(mine, da, jnp.zeros_like(da)), v)
            row_dot = jnp.sum(probs * dprob, axis=-1, keepdims=True)
            ds = (probs * (dprob - row_dot) * scale).astype(bf16)
            dq.append(dot(ds, k))
            dk.append(t_dot(ds, q))
        dq = jnp.where(low, dq[0], dq[1])
        dk = jnp.where(low, dk[0], dk[1])
        dv = jnp.where(low, dv[0], dv[1])
        shifted = slice(lanes.start + wide, lanes.stop + wide)
        dbias_out[0:1, lanes] = jnp.sum(dq, axis=0, keepdims=True)
        dbias_out[0:1, shifted] = jnp.sum(dv, axis=0, keepdims=True)
        low_ref[0, :, lanes] = dq.astype(bf16)
        low_ref[0, :, shifted] = dk.astype(bf16)
        low_ref[1, :, lanes] = dv.astype(bf16)
    a = normed[...]
    dqk_low, dv_low = low_ref[0], low_ref[1, :, :wide]
    g_qk[...] = t_dot(a, dqk_low).astype(bf16).reshape(g_qk.shape)
    deliver_qk = Copies(table, orders[2], dqk, whole_pieces(g_qk), sem_c, True)
    o_grad = t_dot(attended_in[...], middle_low).reshape(n, rows // 2, 2 * wide)
    v_grad = t_dot(a, dv_low).reshape(n, 2, rows // 2, wide)
    for d in range(n):
        top = jnp.concatenate([v_grad[d, 0], v_grad[d, 1]], axis=1)
        g_vo[d] = jnp.concatenate([top, o_grad[d]], axis=0).astype(bf16)
    deliver_vo = Copies(table, orders[3], dvo, whole_pieces(g_vo, down_rows), sem_d, True)
    fetch_qk.wait()
    first = dot_t(dqk_low, merged(wqk)) + dot_t(dv_low, v_weight)
    pfirst_out[...] = first.astype(bf16)
    deliver_qk.wait()
    deliver_vo.wait()


VM = pl.BlockSpec(memory_space=pltpu.VMEM)
SM = pl.BlockSpec(memory_space=pltpu.SMEM)
ANY = pl.BlockSpec(memory_space=pl.ANY)


def shaped(shape, kind):
    return jax.ShapeDtypeStruct(shape, kind)


def launch(kernel, args, outs, scratch):
    call = pl.pallas_call(
        kernel,
        in_specs=[spec for _, spec in args],
        out_specs=[spec for _, _, spec in outs],
        out_shape=[shaped(shape, kind) for shape, kind, _ in outs],
        scratch_shapes=scratch,
    )
    return list(call(*[array for array, _ in args]))


def bound(function, *fixed):
    def kernel(*refs):
        function(*fixed, *refs)

    return kernel


def whole_step(
    tokens, cotangent, lengths, owners, w_qkv, bias_qv, w_out, w_up, bias_up, w_down, vectors
):
    size = lax.axis_size("dp")
    capacity, width = tokens.shape
    wide = w_qkv.shape[-1]
    hidden_units = w_up.shape[-1]
    layers = w_qkv.shape[0]
    rows = width // size
    lined = size == 16
    blocks = size if lined else 1
    parts = 2 if lined else 1
    per = blocks // parts
    far_first = tuple(1 << k for k in range(size.bit_length() - 1))[::-1]
    gathers = GATHERS if lined else [(members, far_first) for members, _ in GATHERS]
    reductions = REDUCTIONS
    if not lined:
        every = [member for members, _ in REDUCTIONS for member in members]
        reductions = [((member,), far_first) for member in every]
    orders = sorted({order for _, order in (*gathers, *reductions)})
    mover = Mover(size, orders)

    def placed(value, count):
        value = jnp.tile(value.reshape(count, -1), (1, size))
        owner = jnp.arange(value.shape[1], dtype=jnp.int32) // (value.shape[1] // size)
        return jnp.where(owner == mover.me, value, jnp.zeros_like(value)).reshape(-1, width)

    small = jnp.concatenate(
        [
            placed(vectors, layers * vectors.shape[1]),
            placed(bias_qv, 2 * layers),
            placed(bias_up, layers),
        ]
    )
    used = small.shape[0]
    tall = -(-used // 8) * 8
    small = jnp.pad(small, ((0, tall - used), (0, 0)))

    qk = [jnp.concatenate([w_qkv[l, 0], w_qkv[l, 1]], axis=1) for l in range(layers)]
    vo = [jnp.concatenate([beside(w_qkv[l, 2]), w_out[l, 0]]) for l in range(layers)]
    up = [below(w_up[l]) for l in range(layers)]
    down = [w_down[l, 0] for l in range(layers)]
    own_blocks = (qk, vo, up, down)

    places = {}
    for members, bits in gathers:
        pieces = [own_blocks[k][layer] for k, layer in members]
        block = pieces[0] if len(pieces) == 1 else jnp.concatenate(pieces)
        order = orders.index(bits)
        pair = mover.gather(block, order)
        begin = 0
        for member, piece in zip(members, pieces):
            places[member] = (pair, order, begin)
            begin += piece.shape[0]
    small = mover.everywhere(small, far_first).astype(f32)

    if lined:
        table = jnp.stack(mover.tables)
    else:
        table = jnp.zeros((1, 1), jnp.int32)

    def natural(k, pair, order, begin):
        if lined:
            return list(pair), begin, order
        many = rows if k < 2 else 2 * rows
        value = jnp.concatenate([part[:, begin : begin + many] for part in pair])
        value = mover.absolute(value, order)
        if k == 1:
            v = below(value[:, : rows // 2]).reshape(width, wide)
            value = jnp.concatenate([beside(v), value[:, rows // 2 :].reshape(wide, width)])
        elif k == 2:
            value = value.reshape(size, 2, rows, width).transpose(1, 0, 2, 3)
        return [value.reshape(1, -1, width)], 0, 0

    weights = [[natural(k, *places[k, l]) for k in range(4)] for l in range(layers)]
    reduced = {
        member: (number, orders.index(bits), len(members))
        for number, (members, bits) in enumerate(reductions)
        for member in members
    }
    part_shapes = [(per, (1 + k // 2) * (width // blocks), width) for k in range(4)]
    shapes = [
        (blocks, width // blocks, width),
        (blocks, width // blocks, width),
        (2, blocks, width // blocks, width),
        (blocks, 2 * (width // blocks), width),
    ]

    segment_ids = slot_segments(lengths, owners, mover.me, capacity)
    live = (segment_ids < lengths.shape[0]).astype(f32)[:, None]
    seg_col, seg_row = segment_ids[:, None], segment_ids[None, :]

    def sems(*ks):
        return [pltpu.SemaphoreType.DMA(((1 + (k == 2)) * blocks,)) for k in ks]

    def holds(*ks):
        return [pltpu.VMEM(shapes[k], bf16) for k in ks]

    def swap(value):
        return lax.ppermute(value, "tensor", [(0, 1), (1, 0)])

    act = (capacity, width)
    tab = [(table, SM)]

    def vm(*arrays):
        return [(array, VM) for array in arrays]

    def hb(layer, *ks):
        return [(array, ANY) for k in ks for array in weights[layer][k][0]]

    def fixed(layer, *ks):
        fetched = tuple(weights[layer][k][2] for k in ks)
        sent = tuple(reduced[k, layer][1] if lined else 0 for k in ks)
        return layer, layers, parts, fetched + sent, tuple(weights[layer][k][1] for k in ks)

    def grad_outs(*ks):
        return [(part_shapes[k], bf16, ANY) for k in ks for _ in range(parts)]

    def attention_forward(layer, inputs):
        outs = [
            (act, bf16, VM),
            ((3, capacity, wide), bf16, VM),
            ((capacity, wide), bf16, VM),
            (act, f32, VM),
        ]
        if layer:
            outs = [(act, f32, VM)] + outs
        return launch(
            bound(attention_forward_kernel, *fixed(layer, 0, 1)),
            tab + vm(*inputs, small, seg_col, seg_row) + hb(layer, 0, 1),
            outs,
            holds(0, 1) + sems(0, 1),
        )

    normed0, qkv0, attended0, own = attention_forward(0, (tokens,))
    other = swap(own)
    middle0, second0, active0, own = launch(
        bound(ffn_forward_kernel, *fixed(0, 2, 3)),
        tab + vm(tokens, own, other, small) + hb(0, 2, 3),
        [
            (act, f32, VM),
            (act, bf16, VM),
            ((capacity, hidden_units), bf16, VM),
            (act, f32, VM),
        ],
        holds(2, 3) + sems(2, 3),
    )
    other = swap(own)
    hidden1, normed1, qkv1, attended1, own = attention_forward(1, (middle0, own, other))
    other = swap(own)

    outs = launch(
        bound(ffn_turn_kernel, *fixed(1, 2, 3)),
        tab + vm(hidden1, own, other, small, cotangent, live) + hb(1, 2, 3),
        [
            (act, f32, VM),
            (act, f32, VM),
            (act, bf16, VM),
            ((hidden_units // width, width), f32, VM),
            ((1, width), f32, VM),
        ]
        + grad_outs(2, 3),
        holds(2, 3, 2, 3) + sems(2, 3, 2, 3),
    )
    middle1, down_own, psec, dbup1, dshift1 = outs[:5]
    dup1, ddown1 = outs[5 : 5 + parts], outs[5 + parts :]

    def summed(k, layer, grads):
        _, order, _ = reduced[k, layer]
        if lined:
            return mover.reduce(grads, order)
        value = grads[0][0]
        if k == 1:
            v = below(value[:wide]).reshape(size, rows, wide)
            value = jnp.concatenate([beside(v), value[wide:].reshape(size, -1, width)], axis=1)
        elif k == 2:
            value = value.reshape(2, size, rows, width).transpose(1, 0, 2, 3)
        value = jnp.take(value.reshape(size, -1, width), mover.tables[order], axis=0)
        return mover.reduce((value[: size // 2], value[size // 2 :]), order)

    def summed_attention(layer, dqk, dvo):
        first = summed(0, layer, dqk)
        if dvo:
            return first, summed(1, layer, dvo)
        return first[:rows], first[rows:]

    up1, down1 = summed(2, 1, dup1), summed(3, 1, ddown1)
    psec_other = swap(psec)
    down_other = swap(down_own)

    def attention_backward(layer, inputs, psec, psec_other, middle, attended, qkv, normed):
        apart = reduced[0, layer][2] == 1
        many = width // blocks
        sent = grad_outs(0, 1)
        if not apart:
            sent = [((per, 2 * many, width), bf16, ANY) for _ in range(parts)]
        outs = launch(
            bound(attention_backward_kernel, apart, many, *fixed(layer, 0, 1)),
            tab
            + vm(*inputs, psec, psec_other, middle, small, attended, qkv, normed)
            + vm(seg_col, seg_row)
            + hb(layer, 0, 1),
            [
                (act, f32, VM),
                (act, bf16, VM),
                ((1, width), f32, VM),
                ((3, width), f32, VM),
            ]
            + sent,
            holds(0, 1, 0, 1)
            + [pltpu.VMEM((2, capacity, width), bf16)]
            + sems(0, 1, 0, 1),
        )
        return outs[:4] + [outs[4 : 4 + parts], outs[4 + parts :]]

    mgrad1, pfirst, dbqv1, dmid1, dqk1, dvo1 = attention_backward(
        1, (cotangent, live), psec, psec_other, middle1, attended1, qkv1, normed1
    )
    qk1, vo1 = summed_attention(1, dqk1, dvo1)
    pfirst_other = swap(pfirst)
    outs = launch(
        bound(ffn_backward_kernel, *fixed(0, 2, 3)),
        tab + vm(mgrad1, pfirst, pfirst_other, hidden1, small, second0, active0)
        + hb(0, 2, 3),
        [
            (act, f32, VM),
            (act, bf16, VM),
            ((hidden_units // width, width), f32, VM),
            ((1, width), f32, VM),
            ((2, width), f32, VM),
        ]
        + grad_outs(2, 3),
        holds(2, 3, 2, 3) + sems(2, 3, 2, 3),
    )
    g0, psec, dbup0, dshift0, dnorm1 = outs[:5]
    dup0, ddown0 = outs[5 : 5 + parts], outs[5 + parts :]
    up0, down0 = summed(2, 0, dup0), summed(3, 0, ddown0)
    psec_other = swap(psec)
    mgrad0, pfirst, dbqv0, dmid0, dqk0, dvo0 = attention_backward(
        0, (g0,), psec, psec_other, middle0, attended0, qkv0, normed0
    )
    qk0, vo0 = summed_attention(0, dqk0, dvo0)
    pfirst_other = swap(pfirst)
    tokens_grad, dnorm0 = launch(
        last_kernel,
        vm(mgrad0, pfirst, pfirst_other, tokens, small),
        [(act, f32, VM), ((2, width), f32, VM)],
        [],
    )

    small_grad = jnp.concatenate(
        [dnorm0, dmid0, dshift0, dnorm1, dmid1, dshift1, dbqv0, dbqv1, dbup0, dbup1]
    )
    small_grad = jnp.pad(small_grad, ((0, tall - used), (0, 0)))
    small_sum = mover.everywhere(small_grad, far_first[::-1])

    def mine(begin, end, count):
        value = small_sum[begin:end].reshape(count, -1)
        many = value.shape[1] // size
        return lax.dynamic_slice(value, (0, mover.me * many), (count, many))

    six = vectors.shape[1] * layers
    vec_sum = mine(0, six, six)
    bqv_sum = mine(six, six + layers, 2 * layers)
    bup_sum = mine(six + layers, used, layers)

    def qkv_of(qk_sum, vo_sum):
        v = below(vo_sum[: rows // 2])
        return jnp.stack([qk_sum[:, :wide], qk_sum[:, wide:], v])

    output = middle1 + ((down_own + down_other) + small[six - 1 : six])
    return (
        output,
        tokens_grad,
        jnp.stack([qkv_of(qk0, vo0), qkv_of(qk1, vo1)]),
        bqv_sum.reshape(bias_qv.shape),
        jnp.stack([vo0[rows // 2 :], vo1[rows // 2 :]]).reshape(w_out.shape),
        jnp.stack([beside(up0), beside(up1)]),
        bup_sum.reshape(bias_up.shape),
        jnp.stack([down0, down1]).reshape(w_down.shape),
        vec_sum.reshape(vectors.shape),
    )


def solution(mesh):
    return sharded(mesh)


def sharded(mesh):
    return jax.shard_map(
        whole_step,
        mesh=mesh,
        in_specs=(
            P("dp", None),
            P("dp", None),
            P(),
            P(),
            P(None, None, "dp", "tensor"),
            P(None, None, "tensor", "dp"),
            P(None, "tensor", "dp", None),
            P(None, "dp", "tensor"),
            P(None, "tensor", "dp"),
            P(None, "tensor", "dp", None),
            P(None, None, "dp"),
        ),
        out_specs=(
            P("dp", None),
            P("dp", None),
            P(None, None, "dp", "tensor"),
            P(None, None, "tensor", "dp"),
            P(None, "tensor", "dp", None),
            P(None, "dp", "tensor"),
            P(None, "tensor", "dp"),
            P(None, "tensor", "dp", None),
            P(None, None, "dp"),
        ),
        check_vma=False,
    )
```
